512 devices in a mesh: cuts: 32 (over z, y_hi), angle: 16 (over y_lo, x, core).
Axes of the slice: x: 4, y: 4 (y_hi: 2, y_lo: 2; y = y_hi * 2 + y_lo), z: 16, core: 2. Of those that a mesh axis runs over, the one named last changes fastest.
Arguments:
- density: bfloat16 [32, 576, 256], P('cuts', 'angle'), may hold values from 0.049804688 to 2
- kernel_blocks: bfloat16 [576, 256, 384], P('cuts'), may hold values from -0.015625 to 0.015625
Outputs:
- sinogram: bfloat16 [32, 576, 384], P('cuts', 'angle')
The draws below stay inside these ranges and needn't reach their ends.
All inputs are finite; a program needn't handle non-finite values.
Results may differ from the reference program's by a relative error of at most 0.0012.
Values may be sent and summed in bfloat16 or wider, within the bound.
No kernel may reach another device: no remote copies, remote signals or barrier semaphores. Data moves between devices by JAX's collectives and lax.ppermute only.
A program may use at most 64 MiB of HBM per device.

```python
import math
import jax
import jax.numpy as jnp

NA = 576
R = 256
B = 384
SLICES = 32


def block_scale(key, shape, shards, low, high):
    def one(axis_at, parts):
        draws = jax.random.uniform(jax.random.fold_in(jax.random.fold_in(key, 6), axis_at), (parts,), jnp.float32, low / len(shards), high / len(shards))
        return jnp.repeat(jnp.exp(draws), shape[axis_at] // parts).reshape((-1,) + (1,) * (len(shape) - axis_at - 1))

    factor_of = one(*shards[0])
    for cut in shards[1:]:
        factor_of = factor_of * one(*cut)
    return factor_of


def bell_draw(own_key, extent, spread, bound, cuts=(), dtype=jnp.bfloat16):
    array = jax.random.normal(own_key, extent, jnp.float32) * spread
    if len(cuts) > 0:
        array = block_scale(own_key, extent, cuts, -0.22, 0.18) * array
    return jnp.clip(array, min=-bound, max=bound).astype(dtype)


def setup_inputs(seed: int = 0) -> dict:
    seeds = jax.random.split(jax.random.key(seed), 3)
    density = jnp.clip(jnp.exp(math.log(2.0) - 3.6927934 * jax.random.uniform(seeds[0], (SLICES, NA, R), jnp.float32) ** block_scale(seeds[0], (SLICES, NA, R), ((0, 32), (1, 16)), -0.2, 0.2)), 0.049804688, 2.0).astype(jnp.bfloat16)
    kernel_blocks = bell_draw(seeds[1], (NA, R, B), (NA * R) ** -0.5, 0.015625, ((0, 32),))
    return {"density": density, "kernel_blocks": kernel_blocks}


def reference(density, kernel_blocks):
    spectrum_image = jnp.fft.rfft(density.astype(jnp.float32), axis=1)
    spectrum_kernel = jnp.fft.rfft(kernel_blocks.astype(jnp.float32), axis=0)
    product_freq = jnp.einsum("skr,krb->skb", spectrum_image, spectrum_kernel)
    contribution = jnp.fft.irfft(product_freq, n=NA, axis=1)
    return contribution.astype(jnp.bfloat16)
```

```python
import jax
import jax.numpy as jnp
from jax import lax
from jax.experimental import pallas as pl
from jax.experimental.pallas import tpu as pltpu
from jax.sharding import Mesh, PartitionSpec as P

CUTS = ("z", "yh")
ANGLE = ("yl", "x", "co")
NZ, NA, NR, NB = 16, 16, 16, 24
LANES = 128
F32, BF16 = jnp.float32, jnp.bfloat16


def rotate(tile, shift):
    shift %= LANES
    return tile if shift == 0 else pltpu.roll(tile, shift, 1)


def assemble(tiles, pieces, lane):
    cache = {}
    for get, src, dst, width in pieces:
        while width > 0:
            step = min(width, LANES - src % LANES, LANES - dst % LANES)
            shift = (dst - src) % LANES
            key = (id(get), src // LANES, shift)
            if key not in cache:
                cache[key] = rotate(get(src // LANES), shift)
            t, at = dst // LANES, dst % LANES
            if tiles[t] is None or step == LANES:
                tiles[t] = cache[key]
            else:
                tiles[t] = jnp.where((lane >= at) & (lane < at + step), cache[key], tiles[t])
            src, dst, width = src + step, dst + step, width - step
    return tiles


def pack_kernel(index_ref, k_ref, o_ref):
    del index_ref
    offsets = k_ref.shape[0]
    lane = lax.broadcasted_iota(jnp.int32, (NR, LANES), 1)
    cache = {}

    def reader(l):
        def get(t):
            if (l, t) not in cache:
                cache[l, t] = k_ref[l, :, t * LANES : (t + 1) * LANES].astype(F32)
            return cache[l, t]

        return get

    readers = [reader(l) for l in range(offsets)]
    width = offsets * NB
    for z in range(NZ):
        tiles = assemble(
            [None] * -(-width // LANES), [(readers[l], z * NB, l * NB, NB) for l in range(offsets)], lane
        )
        for t, tile in enumerate(tiles):
            w = min(LANES, width - t * LANES)
            o_ref[z, :, t * LANES : t * LANES + w] = tile[:, :w].astype(BF16)


def main_kernel(yh_ref, k1_ref, k2_ref, d_ref, o_ref, flat, weights, left, acc):
    half = k1_ref.shape[2]
    blocks = 2 * NZ * half // (NR * NB)
    tiles_all = 2 * NZ * half // LANES
    group = NR * NB // LANES
    lane = lax.broadcasted_iota(jnp.int32, (NR, LANES), 1)
    first = yh_ref[0] == 0

    def reader(z, h):
        cache = {}

        def get(t):
            if t not in cache:
                w = min(LANES, half - t * LANES)
                a = k1_ref[z, :, t * LANES : t * LANES + w].astype(F32)
                b = k2_ref[z, :, t * LANES : t * LANES + w].astype(F32)
                v = jnp.where(first, a, b) if h == 0 else jnp.where(first, b, a)
                if w < LANES:
                    v = jnp.concatenate([v, jnp.zeros((NR, LANES - w), F32)], axis=1)
                cache[t] = v
            return cache[t]

        return get

    tiles = assemble(
        [None] * tiles_all,
        [(reader(z, h), 0, (2 * z + h) * half, half) for z in range(NZ) for h in range(2)],
        lane,
    )
    for t in range(tiles_all):
        flat[t + group] = tiles[t]
    for t in range(group):
        flat[t] = tiles[tiles_all - group + t]

    for w in range(blocks):
        for t in range(2):
            for rep in range(2):
                left[(rep * blocks + w) * NZ : (rep * blocks + w + 1) * NZ, t * LANES : (t + 1) * LANES] = d_ref[2 * w + t]

    def build(block, carry):
        for j in range(NR):
            q, rem = divmod(NB * j, LANES)
            for t in range(group):
                at = block * group + t + group - q
                tile = flat[at]
                if rem:
                    tile = jnp.where(lane >= rem, rotate(tile, rem), rotate(flat[at - 1], rem))
                weights[block, j * NR : (j + 1) * NR, t * LANES : (t + 1) * LANES] = tile.astype(BF16)
        return carry

    lax.fori_loop(0, blocks, build, 0)
    acc[...] = jnp.zeros_like(acc)

    def step(block, carry):
        start = pl.multiple_of((blocks - block) * NZ, NZ)
        acc[...] += jnp.dot(left[pl.ds(start, blocks * NZ), :], weights[block], preferred_element_type=F32)
        return carry

    lax.fori_loop(0, blocks, step, 0)

    width = o_ref.shape[2]

    def out_tile(t):
        return acc[(t // group) * NZ : (t // group + 1) * NZ, (t % group) * LANES : (t % group + 1) * LANES]

    for a in range(NA):
        tiles = assemble([None] * -(-width // LANES), [(out_tile, a * width, 0, width)], lane)
        for t, tile in enumerate(tiles):
            w = min(LANES, width - t * LANES)
            o_ref[a, :, t * LANES : t * LANES + w] = tile[:, :w]


def pack(kernel_blocks, index):
    offsets, _, bins = kernel_blocks.shape
    return pl.pallas_call(
        pack_kernel,
        grid_spec=pltpu.PrefetchScalarGridSpec(
            num_scalar_prefetch=1,
            grid=(1,),
            in_specs=[pl.BlockSpec((offsets, NR, bins), lambda i, index: (0, index[0], 0))],
            out_specs=pl.BlockSpec((NZ, NR, offsets * NB), lambda i, index: (0, 0, 0)),
        ),
        out_shape=jax.ShapeDtypeStruct((NZ, NR, offsets * NB), BF16),
        compiler_params=pltpu.CompilerParams(vmem_limit_bytes=40 << 20),
        name="pack",
    )(index, kernel_blocks)


def project(yh, k1, k2, d):
    half = k1.shape[2]
    blocks = 2 * NZ * half // (NR * NB)
    width = 2 * NZ * half // NA
    vmem = pl.BlockSpec(memory_space=pltpu.VMEM)
    return pl.pallas_call(
        main_kernel,
        in_specs=[pl.BlockSpec(memory_space=pltpu.SMEM), vmem, vmem, vmem],
        out_specs=vmem,
        out_shape=jax.ShapeDtypeStruct((NA, NZ, width), F32),
        scratch_shapes=[
            pltpu.VMEM((2 * NZ * half // LANES + NR * NB // LANES, NR, LANES), F32),
            pltpu.VMEM((blocks, NR * NR, NR * NB), BF16),
            pltpu.VMEM((2 * blocks * NZ, NR * NR), BF16),
            pltpu.VMEM((blocks * NZ, NR * NB), F32),
        ],
        compiler_params=pltpu.CompilerParams(vmem_limit_bytes=40 << 20),
        name="project",
    )(yh, k1, k2, d)


def local(density, kernel_blocks):
    angles = density.shape[1]
    me = lax.axis_index(ANGLE).astype(jnp.int32).reshape(1)
    yh = lax.axis_index("yh").astype(jnp.int32).reshape(1)
    k1 = lax.all_to_all(pack(kernel_blocks, me), "z", 0, 0, tiled=True)
    k2 = lax.ppermute(k1, "yh", [(0, 1), (1, 0)])
    d = density.reshape(angles, NA, NR).transpose(1, 0, 2).reshape(NA, angles * NR)
    d = lax.all_to_all(d, ANGLE, 0, 0, tiled=True)
    d = d.reshape(1, -1, LANES)
    d = lax.all_to_all(jnp.broadcast_to(d, (NZ,) + d.shape[1:]), "z", 0, 0, tiled=True)
    d = d.transpose(1, 0, 2)
    parts = project(yh, k1, k2, d)
    parts = lax.all_to_all(parts, ANGLE, 0, 0, tiled=True)
    out = jnp.sum(parts, axis=0).astype(BF16)
    out = lax.all_to_all(out, "z", 0, 0, tiled=True)
    return out.reshape(NZ, angles, NB).transpose(1, 0, 2).reshape(1, angles, NZ * NB)


def solution(mesh):
    own = Mesh(mesh.devices.reshape(16, 2, 2, 4, 2), CUTS + ANGLE)
    return jax.shard_map(
        local,
        mesh=own,
        in_specs=(P(CUTS, ANGLE, None), P(CUTS, None, None)),
        out_specs=P(CUTS, ANGLE, None),
        check_vma=False,
    )
```

```python
import jax
import jax.numpy as jnp
from jax import lax
from jax.experimental import pallas as pl
from jax.experimental.pallas import tpu as pltpu
from jax.sharding import Mesh, PartitionSpec as P

CUTS = ("z", "yh")
ANGLE = ("yl", "x", "co")
NZ, NA, NR, NB = 16, 16, 16, 24
ROWS, LANES = 16, 128
F32, BF16 = jnp.float32, jnp.bfloat16
VMEM_BYTES = 40 << 20


def rotate(tile, shift):
    shift %= LANES
    return tile if shift == 0 else pltpu.roll(tile, shift, 1)


def assemble(count, pieces):
    lane = lax.broadcasted_iota(jnp.int32, (ROWS, LANES), 1)
    tiles, cache = [None] * count, {}
    for n, (get, src, dst, width) in enumerate(pieces):
        while width > 0:
            step = min(width, LANES - src % LANES, LANES - dst % LANES)
            key = (id(get), src // LANES, (dst - src) % LANES)
            if key not in cache:
                cache[key] = rotate(get(src // LANES), dst - src)
            t, at = dst // LANES, dst % LANES
            if tiles[t] is None or step == LANES:
                tiles[t] = cache[key]
            else:
                tiles[t] = jnp.where((lane >= at) & (lane < at + step), cache[key], tiles[t])
            src, dst, width = src + step, dst + step, width - step
    return tiles


def cached(load):
    seen = {}

    def get(t):
        if t not in seen:
            seen[t] = load(t)
        return seen[t]

    return get


def density_tiles(angles):
    spots, group = [], 0
    for first in range(0, angles, ROWS):
        count = min(ROWS, angles - first)
        if count == ROWS:
            spots += [(first, count, 0, group, 0), (first, count, 1, group + 1, 0)]
            group += 2
        else:
            assert 2 * count <= ROWS
            spots += [(first, count, 0, group, 0), (first, count, 1, group, count)]
            group += 1
    return spots, group


def pack_kernel(index_ref, k_ref, d_ref, o_ref):
    del index_ref
    offsets, angles = k_ref.shape[0], d_ref.shape[0]
    width = offsets * NB
    groups = -(-width // LANES)
    readers = [
        cached(lambda t, l=l: k_ref[l, :, t * LANES : (t + 1) * LANES].astype(F32)) for l in range(offsets)
    ]
    for z in range(NZ):
        tiles = assemble(groups, [(readers[l], z * NB, l * NB, NB) for l in range(offsets)])
        for t, tile in enumerate(tiles):
            o_ref[z, t] = tile.astype(BF16)
    rows = {}
    for first, count, half, group, row in density_tiles(angles)[0]:
        rows.setdefault(group, []).append(
            d_ref[first : first + count, half * LANES : (half + 1) * LANES].astype(F32)
        )
    for group, parts in rows.items():
        have = sum(p.shape[0] for p in parts)
        if have < ROWS:
            parts = parts + [jnp.zeros((ROWS - have, LANES), F32)]
        tile = (parts[0] if len(parts) == 1 else jnp.concatenate(parts, axis=0)).astype(BF16)
        for z in range(NZ):
            o_ref[z, groups + group] = tile


def regroup_kernel(d_ref, o_ref):
    angles = o_ref.shape[1] * LANES // NR
    spots, _ = density_tiles(36)
    per = LANES // NR
    lane = lax.broadcasted_iota(jnp.int32, (NZ, LANES), 1)
    masks = [(lane >= p * NR) & (lane < (p + 1) * NR) for p in range(per)]
    out = {}
    for first, count, half, group, row in spots:
        for i in range(count):
            t, p = divmod(first + i, per)
            tile = d_ref[group, row + i]
            for k in range(per):
                turned = rotate(tile, (p - k) * NR)
                key = (half * per + k, t)
                out[key] = turned if key not in out else jnp.where(masks[p], turned, out[key])
    del angles
    for (a, t), tile in out.items():
        o_ref[a, t] = tile


def main_kernel(yh_ref, k1_ref, k2_ref, d_ref, o_ref, flat, weights, left):
    half = 18 * NB
    group = NR * NB // LANES
    tiles_all = 2 * NZ * half // LANES
    blocks = tiles_all // group
    width = o_ref.shape[2]
    lane = lax.broadcasted_iota(jnp.int32, (ROWS, LANES), 1)
    first = yh_ref[0] == 0

    def reader(z, h):
        def load(t):
            a, b = k1_ref[z, t].astype(F32), k2_ref[z, t].astype(F32)
            return jnp.where(first, a, b) if h == 0 else jnp.where(first, b, a)

        return cached(load)

    tiles = assemble(
        tiles_all, [(reader(z, h), 0, (2 * z + h) * half, half) for z in range(NZ) for h in range(2)]
    )
    for t in range(tiles_all):
        flat[t + group] = tiles[t]
    for t in range(group):
        flat[t] = tiles[tiles_all - group + t]

    span = width * NR // NB
    tiles = assemble(
        blocks * 2, [(cached(lambda t, a=a: d_ref[a, t].astype(F32)), 0, a * span, span) for a in range(NA)]
    )
    for w in range(blocks):
        for t in range(2):
            tile = tiles[2 * w + t].astype(BF16)
            for rep in range(2):
                row = (rep * blocks + w) * NZ
                left[row : row + NZ, t * LANES : (t + 1) * LANES] = tile

    for block in range(blocks):
        for j in range(NR):
            q, rem = divmod(NB * j, LANES)
            base = block * group + group - q
            if rem:
                turned = [rotate(flat[base + t - 1], rem) for t in range(group + 1)]
                outs = [jnp.where(lane >= rem, turned[t + 1], turned[t]) for t in range(group)]
            else:
                outs = [flat[base + t] for t in range(group)]
            for t in range(group):
                weights[block, j * NR : (j + 1) * NR, t * LANES : (t + 1) * LANES] = outs[t].astype(BF16)
    lhs = [left[(blocks - c) * NZ : (2 * blocks - c) * NZ, :] for c in range(blocks)]
    acc = jnp.dot(
        jnp.concatenate(lhs, axis=1),
        weights[...].reshape(blocks * NR * NR, NR * NB),
        preferred_element_type=F32,
    )

    def out_tile(t):
        return acc[(t // group) * NZ : (t // group + 1) * NZ, (t % group) * LANES : (t % group + 1) * LANES]

    for a in range(NA):
        tiles = assemble(-(-width // LANES), [(out_tile, a * width, 0, width)])
        for t, tile in enumerate(tiles):
            w = min(LANES, width - t * LANES)
            o_ref[a, :, t * LANES : t * LANES + w] = tile[:, :w]


def pack(kernel_blocks, density, index):
    offsets, _, bins = kernel_blocks.shape
    angles, radii = density.shape
    groups = -(-offsets * NB // LANES) + density_tiles(angles)[1]
    return pl.pallas_call(
        pack_kernel,
        grid_spec=pltpu.PrefetchScalarGridSpec(
            num_scalar_prefetch=1,
            grid=(1,),
            in_specs=[
                pl.BlockSpec((offsets, NR, bins), lambda i, index: (0, index[0], 0)),
                pl.BlockSpec((angles, radii), lambda i, index: (0, 0)),
            ],
            out_specs=pl.BlockSpec((NZ, groups, ROWS, LANES), lambda i, index: (0, 0, 0, 0)),
        ),
        out_shape=jax.ShapeDtypeStruct((NZ, groups, ROWS, LANES), BF16),
        compiler_params=pltpu.CompilerParams(vmem_limit_bytes=VMEM_BYTES),
        name="pack",
    )(index, kernel_blocks, density)


def regroup(d):
    vmem = pl.BlockSpec(memory_space=pltpu.VMEM)
    return pl.pallas_call(
        regroup_kernel,
        in_specs=[vmem],
        out_specs=vmem,
        out_shape=jax.ShapeDtypeStruct((NA, d.shape[0], NZ, LANES), BF16),
        compiler_params=pltpu.CompilerParams(vmem_limit_bytes=VMEM_BYTES),
        name="regroup",
    )(d)


def project(yh, k1, k2, d):
    half = 18 * NB
    blocks = 2 * NZ * half // (NR * NB)
    width = 2 * NZ * half // NA
    vmem = pl.BlockSpec(memory_space=pltpu.VMEM)
    return pl.pallas_call(
        main_kernel,
        in_specs=[pl.BlockSpec(memory_space=pltpu.SMEM), vmem, vmem, vmem],
        out_specs=vmem,
        out_shape=jax.ShapeDtypeStruct((NA, NZ, width), F32),
        scratch_shapes=[
            pltpu.VMEM((2 * NZ * half // LANES + NR * NB // LANES, ROWS, LANES), F32),
            pltpu.VMEM((blocks, NR * NR, NR * NB), BF16),
            pltpu.VMEM((2 * blocks * NZ, NR * NR), BF16),
        ],
        compiler_params=pltpu.CompilerParams(vmem_limit_bytes=VMEM_BYTES),
        name="project",
    )(yh, k1, k2, d)


def local(density, kernel_blocks):
    offsets, angles = kernel_blocks.shape[0], density.shape[1]
    me = lax.axis_index(ANGLE).astype(jnp.int32).reshape(1)
    yh = lax.axis_index("yh").astype(jnp.int32).reshape(1)
    both = lax.all_to_all(pack(kernel_blocks, density[0], me), "z", 0, 0, tiled=True)
    groups = -(-offsets * NB // LANES)
    k1 = both[:, :groups]
    k2 = lax.ppermute(k1, "yh", [(0, 1), (1, 0)])
    d = regroup(both[:, groups:].transpose(1, 2, 0, 3))
    d = lax.all_to_all(d, ANGLE, 0, 0, tiled=True)
    parts = project(yh, k1, k2, d)
    parts = lax.all_to_all(parts, ANGLE, 0, 0, tiled=True)
    out = jnp.sum(parts, axis=0).astype(BF16)
    out = lax.all_to_all(out, "z", 0, 0, tiled=True)
    return out.reshape(NZ, angles, NB).transpose(1, 0, 2).reshape(1, angles, NZ * NB)


def solution(mesh):
    own = Mesh(mesh.devices.reshape(16, 2, 2, 4, 2), CUTS + ANGLE)
    return jax.shard_map(
        local,
        mesh=own,
        in_specs=(P(CUTS, ANGLE, None), P(CUTS, None, None)),
        out_specs=P(CUTS, ANGLE, None),
        check_vma=False,
    )
```

```python
import jax
import jax.numpy as jnp
from jax import lax
from jax.experimental import pallas as pl
from jax.experimental.pallas import tpu as pltpu
from jax.sharding import Mesh, PartitionSpec as P

CUTS = ("z", "yh")
ANGLE = ("yl", "x", "co")
NZ, NA, NR, NB = 16, 16, 16, 24
OFFSETS, VIEWS = 18, 36
ROWS, LANES = 16, 128
TAIL = OFFSETS * NB % LANES
F32, BF16 = jnp.float32, jnp.bfloat16
VMEM_BYTES = 40 << 20


def rotate(tile, shift):
    shift %= LANES
    return tile if shift == 0 else pltpu.roll(tile, shift, 1)


def assemble(count, pieces):
    lane = lax.broadcasted_iota(jnp.int32, (ROWS, LANES), 1)
    tiles, cache = [None] * count, {}
    for n, (get, src, dst, width) in enumerate(pieces):
        while width > 0:
            step = min(width, LANES - src % LANES, LANES - dst % LANES)
            key = (id(get), src // LANES, (dst - src) % LANES)
            if key not in cache:
                cache[key] = rotate(get(src // LANES), dst - src)
            t, at = dst // LANES, dst % LANES
            if tiles[t] is None or step == LANES:
                tiles[t] = cache[key]
            else:
                tiles[t] = jnp.where((lane >= at) & (lane < at + step), cache[key], tiles[t])
            src, dst, width = src + step, dst + step, width - step
    return tiles


def cached(load):
    seen = {}

    def get(t):
        if t not in seen:
            seen[t] = load(t)
        return seen[t]

    return get


def pack_kernel(mine_ref, yh_ref, k_hbm, d_hbm, o_ref, k_ref, d_ref, sems):
    radii = pl.ds(pl.multiple_of(mine_ref[0] * NR, NR), NR)
    copies = [
        pltpu.make_async_copy(k_hbm.at[:, radii, :], k_ref, sems.at[0]),
        pltpu.make_async_copy(d_hbm.at[0], d_ref, sems.at[1]),
    ]
    for copy in copies:
        copy.start()
    swap = yh_ref[0] == 1
    copies[1].wait()
    low, high = d_ref[:, :LANES].astype(F32), d_ref[:, LANES:].astype(F32)
    halves = jnp.where(swap, high, low), jnp.where(swap, low, high)
    for n in range(2):
        for h in range(2):
            tile = halves[h][n * ROWS : (n + 1) * ROWS].astype(BF16)
            for z in range(NZ):
                o_ref[z, 4 + 2 * n + h] = tile
    rest = [h[2 * ROWS :] for h in halves]
    copies[0].wait()
    readers = [
        cached(lambda t, l=l: k_ref[l, :, t * LANES : (t + 1) * LANES].astype(F32)) for l in range(OFFSETS)
    ]
    lane = lax.broadcasted_iota(jnp.int32, (ROWS // 2, LANES), 1)
    for z in range(NZ):
        tiles = assemble(4, [(readers[l], z * NB, l * NB, NB) for l in range(OFFSETS)])
        for t in range(3):
            o_ref[z, t] = tiles[t].astype(BF16)
        last = jnp.where(lane < TAIL, tiles[3][: ROWS // 2], rotate(tiles[3][ROWS // 2 :], TAIL))
        o_ref[z, 3] = jnp.concatenate([last] + rest, axis=0).astype(BF16)


def regroup_kernel(d_ref, o_ref):
    per = LANES // NR
    lane = lax.broadcasted_iota(jnp.int32, (NZ, LANES), 1)
    masks = [(lane >= p * NR) & (lane < (p + 1) * NR) for p in range(per)]
    out = {}
    for angle in range(VIEWS):
        n, i = divmod(angle, ROWS)
        t, p = divmod(angle, per)
        for h in range(2):
            tile = d_ref[1 + 2 * n + h, i] if n < 2 else d_ref[0, ROWS // 2 + (VIEWS - 2 * ROWS) * h + i]
            for k in range(per):
                turned = rotate(tile, (p - k) * NR)
                key = (h * per + k, t)
                out[key] = turned if key not in out else jnp.where(masks[p], turned, out[key])
    for (a, t), tile in out.items():
        o_ref[a, t] = tile


def main_kernel(yh_ref, k1_ref, k2_ref, d_ref, o_ref, flat, weights, left):
    half = OFFSETS * NB
    group = NR * NB // LANES
    tiles_all = 2 * NZ * half // LANES
    blocks = tiles_all // group
    width = o_ref.shape[2]
    lane = lax.broadcasted_iota(jnp.int32, (ROWS, LANES), 1)
    first = yh_ref[0] == 0

    def reader(z, h):
        def load(t):
            a, b = k1_ref[z, t].astype(F32), k2_ref[z, t].astype(F32)
            tile = jnp.where(first, a, b) if h == 0 else jnp.where(first, b, a)
            if t == 3:
                tile = tile[: ROWS // 2]
                tile = jnp.concatenate([tile, rotate(tile, -TAIL)], axis=0)
            return tile

        return cached(load)

    tiles = assemble(
        tiles_all, [(reader(z, h), 0, (2 * z + h) * half, half) for z in range(NZ) for h in range(2)]
    )
    for t in range(tiles_all):
        flat[t + group] = tiles[t]
    for t in range(group):
        flat[t] = tiles[tiles_all - group + t]

    span = width * NR // NB
    tiles = assemble(
        blocks * 2, [(cached(lambda t, a=a: d_ref[a, t].astype(F32)), 0, a * span, span) for a in range(NA)]
    )
    for w in range(blocks):
        for t in range(2):
            tile = tiles[2 * w + t].astype(BF16)
            for rep in range(2):
                row = (rep * blocks + w) * NZ
                left[row : row + NZ, t * LANES : (t + 1) * LANES] = tile

    for block in range(blocks):
        for j in range(NR):
            q, rem = divmod(NB * j, LANES)
            base = block * group + group - q
            if rem:
                turned = [rotate(flat[base + t - 1], rem) for t in range(group + 1)]
                outs = [jnp.where(lane >= rem, turned[t + 1], turned[t]) for t in range(group)]
            else:
                outs = [flat[base + t] for t in range(group)]
            for t in range(group):
                weights[block, j * NR : (j + 1) * NR, t * LANES : (t + 1) * LANES] = outs[t].astype(BF16)
    lhs = [left[(blocks - c) * NZ : (2 * blocks - c) * NZ, :] for c in range(blocks)]
    acc = jnp.dot(
        jnp.concatenate(lhs, axis=1),
        weights[...].reshape(blocks * NR * NR, NR * NB),
        preferred_element_type=F32,
    )

    def out_tile(t):
        return acc[(t // group) * NZ : (t // group + 1) * NZ, (t % group) * LANES : (t % group + 1) * LANES]

    for a in range(NA):
        tiles = assemble(-(-width // LANES), [(out_tile, a * width, 0, width)])
        for t, tile in enumerate(tiles):
            w = min(LANES, width - t * LANES)
            o_ref[a, :, t * LANES : t * LANES + w] = tile[:, :w]


def pack(mine, yh, kernel_blocks, density):
    hbm, smem = pl.BlockSpec(memory_space=pltpu.HBM), pl.BlockSpec(memory_space=pltpu.SMEM)
    return pl.pallas_call(
        pack_kernel,
        in_specs=[smem, smem, hbm, hbm],
        out_specs=pl.BlockSpec(memory_space=pltpu.VMEM),
        out_shape=jax.ShapeDtypeStruct((NZ, 8, ROWS, LANES), BF16),
        scratch_shapes=[
            pltpu.VMEM((OFFSETS, NR, NZ * NB), BF16),
            pltpu.VMEM((VIEWS, NA * NR), BF16),
            pltpu.SemaphoreType.DMA((2,)),
        ],
        compiler_params=pltpu.CompilerParams(vmem_limit_bytes=VMEM_BYTES),
        name="pack",
    )(mine, yh, *(pltpu.with_memory_space_constraint(v, pltpu.HBM) for v in (kernel_blocks, density)))


def regroup(d):
    vmem = pl.BlockSpec(memory_space=pltpu.VMEM)
    return pl.pallas_call(
        regroup_kernel,
        in_specs=[vmem],
        out_specs=vmem,
        out_shape=jax.ShapeDtypeStruct((NA, d.shape[0], NZ, LANES), BF16),
        compiler_params=pltpu.CompilerParams(vmem_limit_bytes=VMEM_BYTES),
        name="regroup",
    )(d)


def project(yh, k1, k2, d):
    half = OFFSETS * NB
    blocks = 2 * NZ * half // (NR * NB)
    width = 2 * NZ * half // NA
    vmem = pl.BlockSpec(memory_space=pltpu.VMEM)
    return pl.pallas_call(
        main_kernel,
        in_specs=[pl.BlockSpec(memory_space=pltpu.SMEM), vmem, vmem, vmem],
        out_specs=vmem,
        out_shape=jax.ShapeDtypeStruct((NA, NZ, width), F32),
        scratch_shapes=[
            pltpu.VMEM((2 * NZ * half // LANES + NR * NB // LANES, ROWS, LANES), F32),
            pltpu.VMEM((blocks, NR * NR, NR * NB), BF16),
            pltpu.VMEM((2 * blocks * NZ, NR * NR), BF16),
        ],
        compiler_params=pltpu.CompilerParams(vmem_limit_bytes=VMEM_BYTES),
        name="project",
    )(yh, k1, k2, d)


def local(density, kernel_blocks):
    yh, yl, x, co = (lax.axis_index(name).astype(jnp.int32) for name in ("yh",) + ANGLE)
    mine = ((yl ^ yh) * 4 + x) * 2 + co
    both = lax.all_to_all(pack(mine.reshape(1), yh.reshape(1), kernel_blocks, density), "z", 0, 0, tiled=True)
    k1 = both[:, :4]
    k2 = lax.ppermute(k1, ("yh", "yl"), [(0, 3), (1, 2), (2, 1), (3, 0)])
    d = regroup(both[:, 3:].transpose(1, 2, 0, 3))
    d = lax.all_to_all(d, ANGLE, 0, 0, tiled=True)
    parts = project(yh.reshape(1), k1, k2, d)
    parts = lax.all_to_all(parts, ANGLE, 0, 0, tiled=True)
    out = jnp.sum(parts, axis=0).astype(BF16)
    out = lax.all_to_all(out, "z", 0, 0, tiled=True)
    return out.reshape(NZ, VIEWS, NB).transpose(1, 0, 2).reshape(1, VIEWS, NZ * NB)


def solution(mesh):
    own = Mesh(mesh.devices.reshape(16, 2, 2, 4, 2), CUTS + ANGLE)
    return jax.shard_map(
        local,
        mesh=own,
        in_specs=(P(CUTS, ANGLE, None), P(CUTS, None, None)),
        out_specs=P(CUTS, ANGLE, None),
        check_vma=False,
    )
```

```python
import jax
import jax.numpy as jnp
from jax import lax
from jax.experimental import pallas as pl
from jax.experimental.pallas import tpu as pltpu
from jax.sharding import Mesh, PartitionSpec as P

Z = ("zp", "zb")
CUTS = Z + ("yh",)
ANGLE = ("yl", "x", "co")
NZ, NA, NR, NB = 16, 16, 16, 24
OFFSETS, VIEWS = 18, 36
ROWS, LANES = 16, 128
TAIL = OFFSETS * NB % LANES
PART = VIEWS // 2
F32, BF16 = jnp.float32, jnp.bfloat16
VMEM_BYTES = 40 << 20


def rotate(tile, shift):
    shift %= LANES
    return tile if shift == 0 else pltpu.roll(tile, shift, 1)


def assemble(count, pieces):
    lane = lax.broadcasted_iota(jnp.int32, (ROWS, LANES), 1)
    tiles, cache = [None] * count, {}
    for n, (get, src, dst, width) in enumerate(pieces):
        while width > 0:
            step = min(width, LANES - src % LANES, LANES - dst % LANES)
            key = (id(get), src // LANES, (dst - src) % LANES)
            if key not in cache:
                cache[key] = rotate(get(src // LANES), dst - src)
            t, at = dst // LANES, dst % LANES
            if tiles[t] is None or step == LANES:
                tiles[t] = cache[key]
            else:
                tiles[t] = jnp.where((lane >= at) & (lane < at + step), cache[key], tiles[t])
            src, dst, width = src + step, dst + step, width - step
    return tiles


def cached(load):
    seen = {}

    def get(t):
        if t not in seen:
            seen[t] = load(t)
        return seen[t]

    return get


def pack_kernel(mine_ref, yh_ref, k_hbm, d_hbm, o_ref, k_ref, d_ref, sems):
    radii = pl.ds(pl.multiple_of(mine_ref[0] * NR, NR), NR)
    copies = [
        pltpu.make_async_copy(k_hbm.at[:, radii, :], k_ref, sems.at[0]),
        pltpu.make_async_copy(d_hbm.at[0], d_ref, sems.at[1]),
    ]
    for copy in copies:
        copy.start()
    swap = yh_ref[0] == 1
    copies[1].wait()
    low, high = d_ref[:, :LANES].astype(F32), d_ref[:, LANES:].astype(F32)
    halves = jnp.where(swap, high, low), jnp.where(swap, low, high)
    rest = []
    for b in range(2):
        rows = [half[b * PART : (b + 1) * PART] for half in halves]
        for h in range(2):
            tile = rows[h][:ROWS].astype(BF16)
            for z in range(b, NZ, 2):
                o_ref[z, 4 + h] = tile
        parts = [rotate(rows[q // 2][ROWS:], (1 - q % 2) * LANES // 2) for q in range(4)]
        rest.append(jnp.concatenate(parts + [jnp.zeros((ROWS - 4 * (PART - ROWS), LANES), F32)], axis=0))
    copies[0].wait()
    readers = [
        cached(lambda t, l=l: k_ref[l, :, t * LANES : (t + 1) * LANES].astype(F32)) for l in range(OFFSETS)
    ]
    lane = lax.broadcasted_iota(jnp.int32, (ROWS, LANES), 1)
    for z in range(NZ):
        tiles = assemble(4, [(readers[l], z * NB, l * NB, NB) for l in range(OFFSETS)])
        for t in range(3):
            o_ref[z, t] = tiles[t].astype(BF16)
        o_ref[z, 3] = jnp.where(lane < TAIL, tiles[3], rest[z % 2]).astype(BF16)


def regroup_kernel(d_ref, o_ref):
    per = LANES // NR
    lane = lax.broadcasted_iota(jnp.int32, (NZ, LANES), 1)
    masks = [(lane >= p * NR) & (lane < (p + 1) * NR) for p in range(per)]
    out = {}
    for angle in range(PART):
        t, p = divmod(angle, per)
        for a in range(NA):
            if angle < ROWS:
                tile, at = d_ref[1 + a // per, angle], a % per
            else:
                tile, at = d_ref[0, a // 4 * (PART - ROWS) + angle - ROWS], per // 2 + a % 4
            turned = rotate(tile, (p - at) * NR)
            out[a, t] = turned if (a, t) not in out else jnp.where(masks[p], turned, out[a, t])
    for (a, t), tile in out.items():
        for b in range(2):
            o_ref[b * NA + a, t] = tile


def main_kernel(yh_ref, k1_ref, k2_ref, d_ref, o_ref, flat, weights, left):
    half = OFFSETS * NB
    group = NR * NB // LANES
    tiles_all = 2 * NZ * half // LANES
    blocks = tiles_all // group
    width = o_ref.shape[2]
    lane = lax.broadcasted_iota(jnp.int32, (ROWS, LANES), 1)
    first = yh_ref[0] == 0

    def reader(z, h):
        def load(t):
            a, b = k1_ref[z, t].astype(F32), k2_ref[z, t].astype(F32)
            return jnp.where(first, a, b) if h == 0 else jnp.where(first, b, a)

        return cached(load)

    tiles = assemble(
        tiles_all, [(reader(z, h), 0, (2 * z + h) * half, half) for z in range(NZ) for h in range(2)]
    )
    for t in range(tiles_all):
        flat[t + group] = tiles[t]
    for t in range(group):
        flat[t] = tiles[tiles_all - group + t]

    span = PART * NR
    tiles = assemble(
        blocks * 2,
        [
            (cached(lambda t, n=b * NA + a: d_ref[n, t].astype(F32)), 0, (2 * a + b) * span, span)
            for a in range(NA)
            for b in range(2)
        ],
    )
    for w in range(blocks):
        for t in range(2):
            tile = tiles[2 * w + t].astype(BF16)
            for rep in range(2):
                row = (rep * blocks + w) * NZ
                left[row : row + NZ, t * LANES : (t + 1) * LANES] = tile

    for block in range(blocks):
        for j in range(NR):
            q, rem = divmod(NB * j, LANES)
            base = block * group + group - q
            if rem:
                turned = [rotate(flat[base + t - 1], rem) for t in range(group + 1)]
                outs = [jnp.where(lane >= rem, turned[t + 1], turned[t]) for t in range(group)]
            else:
                outs = [flat[base + t] for t in range(group)]
            for t in range(group):
                weights[block, j * NR : (j + 1) * NR, t * LANES : (t + 1) * LANES] = outs[t].astype(BF16)
    lhs = [left[(blocks - c) * NZ : (2 * blocks - c) * NZ, :] for c in range(blocks)]
    acc = jnp.dot(
        jnp.concatenate(lhs, axis=1),
        weights[...].reshape(blocks * NR * NR, NR * NB),
        preferred_element_type=F32,
    )

    def out_tile(t):
        return acc[(t // group) * NZ : (t // group + 1) * NZ, (t % group) * LANES : (t % group + 1) * LANES]

    for a in range(NA):
        tiles = assemble(-(-width // LANES), [(out_tile, a * width, 0, width)])
        for t, tile in enumerate(tiles):
            w = min(LANES, width - t * LANES)
            o_ref[a, :, t * LANES : t * LANES + w] = tile[:, :w]


def pack(mine, yh, kernel_blocks, density):
    hbm, smem = pl.BlockSpec(memory_space=pltpu.HBM), pl.BlockSpec(memory_space=pltpu.SMEM)
    return pl.pallas_call(
        pack_kernel,
        in_specs=[smem, smem, hbm, hbm],
        out_specs=pl.BlockSpec(memory_space=pltpu.VMEM),
        out_shape=jax.ShapeDtypeStruct((NZ, 6, ROWS, LANES), BF16),
        scratch_shapes=[
            pltpu.VMEM((OFFSETS, NR, NZ * NB), BF16),
            pltpu.VMEM((VIEWS, NA * NR), BF16),
            pltpu.SemaphoreType.DMA((2,)),
        ],
        compiler_params=pltpu.CompilerParams(vmem_limit_bytes=VMEM_BYTES),
        name="pack",
    )(mine, yh, *(pltpu.with_memory_space_constraint(v, pltpu.HBM) for v in (kernel_blocks, density)))


def regroup(d):
    vmem = pl.BlockSpec(memory_space=pltpu.VMEM)
    return pl.pallas_call(
        regroup_kernel,
        in_specs=[vmem],
        out_specs=vmem,
        out_shape=jax.ShapeDtypeStruct((2 * NA, d.shape[0], NZ, LANES), BF16),
        compiler_params=pltpu.CompilerParams(vmem_limit_bytes=VMEM_BYTES),
        name="regroup",
    )(d)


def project(yh, k1, k2, d):
    half = OFFSETS * NB
    blocks = 2 * NZ * half // (NR * NB)
    width = 2 * NZ * half // NA
    vmem = pl.BlockSpec(memory_space=pltpu.VMEM)
    return pl.pallas_call(
        main_kernel,
        in_specs=[pl.BlockSpec(memory_space=pltpu.SMEM), vmem, vmem, vmem],
        out_specs=vmem,
        out_shape=jax.ShapeDtypeStruct((NA, NZ, width), F32),
        scratch_shapes=[
            pltpu.VMEM((2 * NZ * half // LANES + NR * NB // LANES, ROWS, LANES), F32),
            pltpu.VMEM((blocks, NR * NR, NR * NB), BF16),
            pltpu.VMEM((2 * blocks * NZ, NR * NR), BF16),
        ],
        compiler_params=pltpu.CompilerParams(vmem_limit_bytes=VMEM_BYTES),
        name="project",
    )(yh, k1, k2, d)


def local(density, kernel_blocks):
    yh, yl, x, co = (lax.axis_index(name).astype(jnp.int32) for name in ("yh",) + ANGLE)
    mine = ((yl ^ yh) * 4 + x) * 2 + co
    both = lax.all_to_all(pack(mine.reshape(1), yh.reshape(1), kernel_blocks, density), Z, 0, 0, tiled=True)
    k1 = both[:, :4]
    k2 = lax.ppermute(k1, ("yh", "yl"), [(0, 3), (1, 2), (2, 1), (3, 0)])
    d = regroup(both[:, 3:].transpose(1, 2, 0, 3))
    d = lax.all_to_all(d, ("zb",) + ANGLE, 0, 0, tiled=True)
    parts = project(yh.reshape(1), k1, k2, d)
    parts = lax.all_to_all(parts, ANGLE, 0, 0, tiled=True)
    out = jnp.sum(parts, axis=0).astype(BF16)
    out = lax.all_to_all(out, Z, 0, 0, tiled=True)
    return out.reshape(NZ, VIEWS, NB).transpose(1, 0, 2).reshape(1, VIEWS, NZ * NB)


def solution(mesh):
    own = Mesh(mesh.devices.reshape(8, 2, 2, 2, 4, 2), CUTS + ANGLE)
    return jax.shard_map(
        local,
        mesh=own,
        in_specs=(P(CUTS, ANGLE, None), P(CUTS, None, None)),
        out_specs=P(CUTS, ANGLE, None),
        check_vma=False,
    )
```

```python
import jax
import jax.numpy as jnp
from jax import lax
from jax.experimental import pallas as pl
from jax.experimental.pallas import tpu as pltpu
from jax.sharding import Mesh, PartitionSpec as P

Z = ("zp", "zb")
CUTS = Z + ("yh",)
ANGLE = ("yl", "x", "co")
NZ, NA, NR, NB = 16, 16, 16, 24
OFFSETS, VIEWS = 18, 36
ROWS, LANES = 16, 128
TAIL = OFFSETS * NB % LANES
PART = VIEWS // 2
F32, BF16 = jnp.float32, jnp.bfloat16
VMEM_BYTES = 40 << 20


def rotate(tile, shift):
    shift %= LANES
    return tile if shift == 0 else pltpu.roll(tile, shift, 1)


def assemble(count, pieces):
    lane = lax.broadcasted_iota(jnp.int32, (ROWS, LANES), 1)
    tiles, cache = [None] * count, {}
    for n, (get, src, dst, width) in enumerate(pieces):
        while width > 0:
            step = min(width, LANES - src % LANES, LANES - dst % LANES)
            key = (id(get), src // LANES, (dst - src) % LANES)
            if key not in cache:
                cache[key] = rotate(get(src // LANES), dst - src)
            t, at = dst // LANES, dst % LANES
            if tiles[t] is None or step == LANES:
                tiles[t] = cache[key]
            else:
                tiles[t] = jnp.where((lane >= at) & (lane < at + step), cache[key], tiles[t])
            src, dst, width = src + step, dst + step, width - step
    return tiles


def cached(load):
    seen = {}

    def get(t):
        if t not in seen:
            seen[t] = load(t)
        return seen[t]

    return get


def pack_kernel(mine_ref, yh_ref, k_hbm, d_hbm, o_ref, k_ref, d_ref, sems):
    radii = pl.ds(pl.multiple_of(mine_ref[0] * NR, NR), NR)
    copies = [
        pltpu.make_async_copy(k_hbm.at[:, radii, :], k_ref, sems.at[0]),
        pltpu.make_async_copy(d_hbm.at[0], d_ref, sems.at[1]),
    ]
    for copy in copies:
        copy.start()
    swap = yh_ref[0] == 1
    copies[1].wait()
    low, high = d_ref[:, :LANES].astype(F32), d_ref[:, LANES:].astype(F32)
    halves = jnp.where(swap, high, low), jnp.where(swap, low, high)
    rest = []
    for b in range(2):
        rows = [half[b * PART : (b + 1) * PART] for half in halves]
        for h in range(2):
            tile = rows[h][:ROWS].astype(BF16)
            for z in range(b, NZ, 2):
                o_ref[z, 4 + h] = tile
        parts = [rotate(rows[q // 2][ROWS:], (1 - q % 2) * LANES // 2) for q in range(4)]
        rest.append(jnp.concatenate(parts + [jnp.zeros((ROWS - 4 * (PART - ROWS), LANES), F32)], axis=0))
    copies[0].wait()
    readers = [
        cached(lambda t, l=l: k_ref[l, :, t * LANES : (t + 1) * LANES].astype(F32)) for l in range(OFFSETS)
    ]
    lane = lax.broadcasted_iota(jnp.int32, (ROWS, LANES), 1)
    for z in range(NZ):
        tiles = assemble(4, [(readers[l], z * NB, l * NB, NB) for l in range(OFFSETS)])
        for t in range(3):
            o_ref[z, t] = tiles[t].astype(BF16)
        o_ref[z, 3] = jnp.where(lane < TAIL, tiles[3], rest[z % 2]).astype(BF16)


def regroup_kernel(k_ref, d_ref, o_ref, swap_ref):
    per = LANES // NR
    lane = lax.broadcasted_iota(jnp.int32, (NZ, LANES), 1)
    masks = [(lane >= p * NR) & (lane < (p + 1) * NR) for p in range(per)]
    out = {}
    for angle in range(PART):
        t, p = divmod(angle, per)
        for a in range(NA):
            if angle < ROWS:
                tile, at = d_ref[1 + a // per, angle], a % per
            else:
                tile, at = d_ref[0, a // 4 * (PART - ROWS) + angle - ROWS], per // 2 + a % 4
            turned = rotate(tile, (p - at) * NR)
            out[a, t] = turned if (a, t) not in out else jnp.where(masks[p], turned, out[a, t])
    for (a, t), tile in out.items():
        for b in range(2):
            o_ref[b * NA + a, t] = tile
    for z in range(NZ):
        for t in range(3):
            swap_ref[z * 3 + t] = k_ref[z, t]
    for z in range(0, NZ, 2):
        swap_ref[NZ * 3 + z // 2] = jnp.where(lane < TAIL, k_ref[z, 3], rotate(k_ref[z + 1, 3], TAIL))


def main_kernel(yh_ref, co_ref, k1_ref, k2_ref, d_ref, own_ref, other_ref, flat, weights, left):
    half = OFFSETS * NB
    group = NR * NB // LANES
    tiles_all = 2 * NZ * half // LANES
    blocks = tiles_all // group
    width = own_ref.shape[2]
    lane = lax.broadcasted_iota(jnp.int32, (ROWS, LANES), 1)
    first = yh_ref[0] == 0

    def reader(z, h):
        def load(t):
            a = k1_ref[z, t].astype(F32)
            b = k2_ref[z * 3 + t if t < 3 else NZ * 3 + z // 2].astype(F32)
            if t == 3 and z % 2:
                b = rotate(b, -TAIL)
            return jnp.where(first, a, b) if h == 0 else jnp.where(first, b, a)

        return cached(load)

    tiles = assemble(
        tiles_all, [(reader(z, h), 0, (2 * z + h) * half, half) for z in range(NZ) for h in range(2)]
    )
    for t in range(tiles_all):
        flat[t + group] = tiles[t]
    for t in range(group):
        flat[t] = tiles[tiles_all - group + t]

    span = PART * NR
    tiles = assemble(
        blocks * 2,
        [
            (cached(lambda t, n=b * NA + a: d_ref[n, t].astype(F32)), 0, (2 * a + b) * span, span)
            for a in range(NA)
            for b in range(2)
        ],
    )
    for w in range(blocks):
        for t in range(2):
            tile = tiles[2 * w + t].astype(BF16)
            for rep in range(2):
                row = (rep * blocks + w) * NZ
                left[row : row + NZ, t * LANES : (t + 1) * LANES] = tile

    for block in range(blocks):
        for j in range(NR):
            q, rem = divmod(NB * j, LANES)
            base = block * group + group - q
            if rem:
                turned = [rotate(flat[base + t - 1], rem) for t in range(group + 1)]
                outs = [jnp.where(lane >= rem, turned[t + 1], turned[t]) for t in range(group)]
            else:
                outs = [flat[base + t] for t in range(group)]
            for t in range(group):
                weights[block, j * NR : (j + 1) * NR, t * LANES : (t + 1) * LANES] = outs[t].astype(BF16)
    lhs = [left[(blocks - c) * NZ : (2 * blocks - c) * NZ, :] for c in range(blocks)]
    acc = jnp.dot(
        jnp.concatenate(lhs, axis=1),
        weights[...].reshape(blocks * NR * NR, NR * NB),
        preferred_element_type=F32,
    )

    def out_tile(t):
        return acc[(t // group) * NZ : (t // group + 1) * NZ, (t % group) * LANES : (t % group + 1) * LANES]

    one = co_ref[0] == 1
    count = -(-width // LANES)
    for n in range(NA // 2):
        pair = [assemble(count, [(out_tile, a * width, 0, width)]) for a in (2 * n, 2 * n + 1)]
        for t in range(count):
            w = min(LANES, width - t * LANES)
            even, odd = (p[t][:, :w] for p in pair)
            own_ref[n, :, t * LANES : t * LANES + w] = jnp.where(one, odd, even)
            other_ref[n, :, t * LANES : t * LANES + w] = jnp.where(one, even, odd)


def pack(mine, yh, kernel_blocks, density):
    hbm, smem = pl.BlockSpec(memory_space=pltpu.HBM), pl.BlockSpec(memory_space=pltpu.SMEM)
    return pl.pallas_call(
        pack_kernel,
        in_specs=[smem, smem, hbm, hbm],
        out_specs=pl.BlockSpec(memory_space=pltpu.VMEM),
        out_shape=jax.ShapeDtypeStruct((NZ, 6, ROWS, LANES), BF16),
        scratch_shapes=[
            pltpu.VMEM((OFFSETS, NR, NZ * NB), BF16),
            pltpu.VMEM((VIEWS, NA * NR), BF16),
            pltpu.SemaphoreType.DMA((2,)),
        ],
        compiler_params=pltpu.CompilerParams(vmem_limit_bytes=VMEM_BYTES),
        name="pack",
    )(mine, yh, *(pltpu.with_memory_space_constraint(v, pltpu.HBM) for v in (kernel_blocks, density)))


def regroup(both):
    vmem = pl.BlockSpec(memory_space=pltpu.VMEM)
    d = both[:, 3:].transpose(1, 2, 0, 3)
    return pl.pallas_call(
        regroup_kernel,
        in_specs=[vmem, vmem],
        out_specs=[vmem, vmem],
        out_shape=[
            jax.ShapeDtypeStruct((2 * NA, d.shape[0], NZ, LANES), BF16),
            jax.ShapeDtypeStruct((NZ * 3 + NZ // 2, ROWS, LANES), BF16),
        ],
        compiler_params=pltpu.CompilerParams(vmem_limit_bytes=VMEM_BYTES),
        name="regroup",
    )(both, d)


def project(yh, co, k1, k2, d):
    half = OFFSETS * NB
    blocks = 2 * NZ * half // (NR * NB)
    width = 2 * NZ * half // NA
    smem, vmem = pl.BlockSpec(memory_space=pltpu.SMEM), pl.BlockSpec(memory_space=pltpu.VMEM)
    return pl.pallas_call(
        main_kernel,
        in_specs=[smem, smem, vmem, vmem, vmem],
        out_specs=[vmem, vmem],
        out_shape=[jax.ShapeDtypeStruct((NA // 2, NZ, width), F32)] * 2,
        scratch_shapes=[
            pltpu.VMEM((2 * NZ * half // LANES + NR * NB // LANES, ROWS, LANES), F32),
            pltpu.VMEM((blocks, NR * NR, NR * NB), BF16),
            pltpu.VMEM((2 * blocks * NZ, NR * NR), BF16),
        ],
        compiler_params=pltpu.CompilerParams(vmem_limit_bytes=VMEM_BYTES),
        name="project",
    )(yh, co, k1, k2, d)


def local(density, kernel_blocks):
    yh, yl, x, co = (lax.axis_index(name).astype(jnp.int32) for name in ("yh",) + ANGLE)
    mine = ((yl ^ yh) * 4 + x) * 2 + co
    both = lax.all_to_all(pack(mine.reshape(1), yh.reshape(1), kernel_blocks, density), Z, 0, 0, tiled=True)
    d, k2 = regroup(both)
    k2 = lax.ppermute(k2, ("yh", "yl"), [(0, 3), (1, 2), (2, 1), (3, 0)])
    d = lax.all_to_all(d, ("zb",) + ANGLE, 0, 0, tiled=True)
    own, other = project(yh.reshape(1), co.reshape(1), both, k2, d)
    parts = own + lax.ppermute(other, "co", [(0, 1), (1, 0)])
    parts = lax.all_to_all(parts, ("yl", "x"), 0, 0, tiled=True)
    out = jnp.sum(parts, axis=0).astype(BF16)
    out = lax.all_to_all(out, Z, 0, 0, tiled=True)
    return out.reshape(NZ, VIEWS, NB).transpose(1, 0, 2).reshape(1, VIEWS, NZ * NB)


def solution(mesh):
    own = Mesh(mesh.devices.reshape(8, 2, 2, 2, 4, 2), CUTS + ANGLE)
    return jax.shard_map(
        local,
        mesh=own,
        in_specs=(P(CUTS, ANGLE, None), P(CUTS, None, None)),
        out_specs=P(CUTS, ANGLE, None),
        check_vma=False,
    )
```

```python
import jax
import jax.numpy as jnp
from jax import lax
from jax.experimental import pallas as pl
from jax.experimental.pallas import tpu as pltpu
from jax.sharding import Mesh, PartitionSpec as P

Z = ("zp", "zb")
CUTS = Z + ("yh",)
ANGLE = ("yl", "x", "co")
NZ, NA, NR, NB = 16, 16, 16, 24
OFFSETS, VIEWS = 18, 36
ROWS, LANES = 16, 128
TAIL = OFFSETS * NB % LANES
PART = VIEWS // 2
F32, BF16 = jnp.float32, jnp.bfloat16
VMEM_BYTES = 40 << 20


def rotate(tile, shift):
    shift %= LANES
    return tile if shift == 0 else pltpu.roll(tile, shift, 1)


def assemble(count, pieces):
    lane = lax.broadcasted_iota(jnp.int32, (ROWS, LANES), 1)
    tiles, cache = [None] * count, {}
    for n, (get, src, dst, width) in enumerate(pieces):
        while width > 0:
            step = min(width, LANES - src % LANES, LANES - dst % LANES)
            key = (id(get), src // LANES, (dst - src) % LANES)
            if key not in cache:
                cache[key] = rotate(get(src // LANES), dst - src)
            t, at = dst // LANES, dst % LANES
            if tiles[t] is None or step == LANES:
                tiles[t] = cache[key]
            else:
                tiles[t] = jnp.where((lane >= at) & (lane < at + step), cache[key], tiles[t])
            src, dst, width = src + step, dst + step, width - step
    return tiles


def cached(load):
    seen = {}

    def get(t):
        if t not in seen:
            seen[t] = load(t)
        return seen[t]

    return get


def pack_kernel(mine_ref, yh_ref, k_hbm, d_hbm, o_ref, k_ref, d_ref, sems):
    radii = pl.ds(pl.multiple_of(mine_ref[0] * NR, NR), NR)
    copies = [
        pltpu.make_async_copy(k_hbm.at[:, radii, :], k_ref, sems.at[0]),
        pltpu.make_async_copy(d_hbm.at[0], d_ref, sems.at[1]),
    ]
    for copy in copies:
        copy.start()
    swap = yh_ref[0] == 1
    copies[1].wait()
    low, high = d_ref[:, :LANES].astype(F32), d_ref[:, LANES:].astype(F32)
    halves = jnp.where(swap, high, low), jnp.where(swap, low, high)
    rest = []
    for b in range(2):
        rows = [half[b * PART : (b + 1) * PART] for half in halves]
        for h in range(2):
            tile = rows[h][:ROWS].astype(BF16)
            for z in range(b, NZ, 2):
                o_ref[z, 4 + h] = tile
        parts = [rotate(rows[q // 2][ROWS:], (1 - q % 2) * LANES // 2) for q in range(4)]
        rest.append(jnp.concatenate(parts + [jnp.zeros((ROWS - 4 * (PART - ROWS), LANES), F32)], axis=0))
    copies[0].wait()
    readers = [
        cached(lambda t, l=l: k_ref[l, :, t * LANES : (t + 1) * LANES].astype(F32)) for l in range(OFFSETS)
    ]
    lane = lax.broadcasted_iota(jnp.int32, (ROWS, LANES), 1)
    for z in range(NZ):
        tiles = assemble(4, [(readers[l], z * NB, l * NB, NB) for l in range(OFFSETS)])
        for t in range(3):
            o_ref[z, t] = tiles[t].astype(BF16)
        o_ref[z, 3] = jnp.where(lane < TAIL, tiles[3], rest[z % 2]).astype(BF16)


def regroup_kernel(k_ref, d_ref, o_ref, swap_ref):
    per = LANES // NR
    lane = lax.broadcasted_iota(jnp.int32, (NZ, LANES), 1)
    masks = [(lane >= p * NR) & (lane < (p + 1) * NR) for p in range(per)]
    out = {}
    for angle in range(PART):
        t, p = divmod(angle, per)
        for a in range(NA):
            if angle < ROWS:
                tile, at = d_ref[1 + a // per, angle], a % per
            else:
                tile, at = d_ref[0, a // 4 * (PART - ROWS) + angle - ROWS], per // 2 + a % 4
            turned = rotate(tile, (p - at) * NR)
            out[a, t] = turned if (a, t) not in out else jnp.where(masks[p], turned, out[a, t])
    for (a, t), tile in out.items():
        for b in range(2):
            o_ref[b * NA + a, t] = tile
    for z in range(NZ):
        for t in range(3):
            swap_ref[z * 3 + t] = k_ref[z, t]
    for z in range(0, NZ, 2):
        swap_ref[NZ * 3 + z // 2] = jnp.where(lane < TAIL, k_ref[z, 3], rotate(k_ref[z + 1, 3], TAIL))


def main_kernel(yh_ref, co_ref, k1_ref, k2_ref, d_ref, own_ref, other_ref, flat, weights, paired, left):
    half = OFFSETS * NB
    group = NR * NB // LANES
    tiles_all = 2 * NZ * half // LANES
    blocks = tiles_all // group
    width = own_ref.shape[2]
    lane = lax.broadcasted_iota(jnp.int32, (ROWS, LANES), 1)
    first = yh_ref[0] == 0

    def reader(z, h):
        def load(t):
            a = k1_ref[z, t].astype(F32)
            b = k2_ref[z * 3 + t if t < 3 else NZ * 3 + z // 2].astype(F32)
            if t == 3 and z % 2:
                b = rotate(b, -TAIL)
            return jnp.where(first, a, b) if h == 0 else jnp.where(first, b, a)

        return cached(load)

    tiles = assemble(
        tiles_all, [(reader(z, h), 0, (2 * z + h) * half, half) for z in range(NZ) for h in range(2)]
    )
    for t in range(tiles_all):
        flat[t + group] = tiles[t]
    for t in range(group):
        flat[t] = tiles[tiles_all - group + t]

    span = PART * NR
    tiles = assemble(
        blocks * 2,
        [
            (cached(lambda t, n=b * NA + a: d_ref[n, t].astype(F32)), 0, (2 * a + b) * span, span)
            for a in range(NA)
            for b in range(2)
        ],
    )
    for w in range(blocks):
        for t in range(2):
            tile = tiles[2 * w + t].astype(BF16)
            for rep in range(2):
                row = (rep * blocks + w) * NZ
                left[row : row + NZ, t * LANES : (t + 1) * LANES] = tile

    for block in range(blocks):
        for j in range(NR):
            q, rem = divmod(NB * j, LANES)
            base = block * group + group - q
            if rem:
                turned = [rotate(flat[base + t - 1], rem) for t in range(group + 1)]
                outs = [jnp.where(lane >= rem, turned[t + 1], turned[t]) for t in range(group)]
            else:
                outs = [flat[base + t] for t in range(group)]
            rows = slice(block * NR * NR + j * NR, block * NR * NR + (j + 1) * NR)
            for t in range(group - 1):
                weights[rows, t * LANES : (t + 1) * LANES] = outs[t].astype(BF16)
            pair, side = divmod(block, 2)
            rows = slice(pair * NR * NR + j * NR, pair * NR * NR + (j + 1) * NR)
            paired[rows, side * LANES : (side + 1) * LANES] = outs[group - 1].astype(BF16)
    lhs = [left[(blocks - c) * NZ : (2 * blocks - c) * NZ, :] for c in range(blocks)]
    acc = jnp.dot(jnp.concatenate(lhs, axis=1), weights[...], preferred_element_type=F32)
    last = jnp.dot(jnp.concatenate(lhs[::2], axis=1), paired[...], preferred_element_type=F32)

    def tile_of(t):
        u, t = divmod(t, group)
        if t < group - 1:
            return acc[u * NZ : (u + 1) * NZ, t * LANES : (t + 1) * LANES]
        before = (u - 1) % blocks
        return last[u * NZ : (u + 1) * NZ, :LANES] + last[before * NZ : (before + 1) * NZ, LANES:]

    out_tile = cached(tile_of)
    one = co_ref[0] == 1
    count = -(-width // LANES)
    for n in range(NA // 2):
        pair = [assemble(count, [(out_tile, a * width, 0, width)]) for a in (2 * n, 2 * n + 1)]
        for t in range(count):
            w = min(LANES, width - t * LANES)
            even, odd = (p[t][:, :w] for p in pair)
            own_ref[n, :, t * LANES : t * LANES + w] = jnp.where(one, odd, even)
            other_ref[n, :, t * LANES : t * LANES + w] = jnp.where(one, even, odd)


def fold_kernel(p_ref, o_ref, rows):
    width = p_ref.shape[2]
    rows[...] = jnp.zeros_like(rows)
    for t in range(-(-width // LANES)):
        w = min(LANES, width - t * LANES)
        tile = p_ref[0, :, t * LANES : t * LANES + w]
        for n in range(1, p_ref.shape[0]):
            tile = tile + p_ref[n, :, t * LANES : t * LANES + w]
        rows[:, t, :w] = tile
    o_ref[...] = rows[...].astype(BF16)


def pack(mine, yh, kernel_blocks, density):
    hbm, smem = pl.BlockSpec(memory_space=pltpu.HBM), pl.BlockSpec(memory_space=pltpu.SMEM)
    return pl.pallas_call(
        pack_kernel,
        in_specs=[smem, smem, hbm, hbm],
        out_specs=pl.BlockSpec(memory_space=pltpu.VMEM),
        out_shape=jax.ShapeDtypeStruct((NZ, 6, ROWS, LANES), BF16),
        scratch_shapes=[
            pltpu.VMEM((OFFSETS, NR, NZ * NB), BF16),
            pltpu.VMEM((VIEWS, NA * NR), BF16),
            pltpu.SemaphoreType.DMA((2,)),
        ],
        compiler_params=pltpu.CompilerParams(vmem_limit_bytes=VMEM_BYTES),
        name="pack",
    )(mine, yh, *(pltpu.with_memory_space_constraint(v, pltpu.HBM) for v in (kernel_blocks, density)))


def regroup(both):
    vmem = pl.BlockSpec(memory_space=pltpu.VMEM)
    d = both[:, 3:].transpose(1, 2, 0, 3)
    return pl.pallas_call(
        regroup_kernel,
        in_specs=[vmem, vmem],
        out_specs=[vmem, vmem],
        out_shape=[
            jax.ShapeDtypeStruct((2 * NA, d.shape[0], NZ, LANES), BF16),
            jax.ShapeDtypeStruct((NZ * 3 + NZ // 2, ROWS, LANES), BF16),
        ],
        compiler_params=pltpu.CompilerParams(vmem_limit_bytes=VMEM_BYTES),
        name="regroup",
    )(both, d)


def project(yh, co, k1, k2, d):
    half = OFFSETS * NB
    blocks = 2 * NZ * half // (NR * NB)
    width = 2 * NZ * half // NA
    smem, vmem = pl.BlockSpec(memory_space=pltpu.SMEM), pl.BlockSpec(memory_space=pltpu.VMEM)
    return pl.pallas_call(
        main_kernel,
        in_specs=[smem, smem, vmem, vmem, vmem],
        out_specs=[vmem, vmem],
        out_shape=[jax.ShapeDtypeStruct((NA // 2, NZ, width), F32)] * 2,
        scratch_shapes=[
            pltpu.VMEM((2 * NZ * half // LANES + NR * NB // LANES, ROWS, LANES), F32),
            pltpu.VMEM((blocks * NR * NR, 2 * LANES), BF16),
            pltpu.VMEM((blocks // 2 * NR * NR, 2 * LANES), BF16),
            pltpu.VMEM((2 * blocks * NZ, NR * NR), BF16),
        ],
        compiler_params=pltpu.CompilerParams(vmem_limit_bytes=VMEM_BYTES),
        name="project",
    )(yh, co, k1, k2, d)


def fold(parts):
    vmem = pl.BlockSpec(memory_space=pltpu.VMEM)
    return pl.pallas_call(
        fold_kernel,
        in_specs=[vmem],
        out_specs=vmem,
        out_shape=jax.ShapeDtypeStruct((NZ, 8, LANES), BF16),
        scratch_shapes=[pltpu.VMEM((NZ, 8, LANES), F32)],
        compiler_params=pltpu.CompilerParams(vmem_limit_bytes=VMEM_BYTES),
        name="fold",
    )(parts)


def local(density, kernel_blocks):
    yh, yl, x, co = (lax.axis_index(name).astype(jnp.int32) for name in ("yh",) + ANGLE)
    mine = ((yl ^ yh) * 4 + x) * 2 + co
    both = lax.all_to_all(pack(mine.reshape(1), yh.reshape(1), kernel_blocks, density), Z, 0, 0, tiled=True)
    d, k2 = regroup(both)
    k2 = lax.ppermute(k2, ("yh", "yl"), [(0, 3), (1, 2), (2, 1), (3, 0)])
    d = lax.all_to_all(d, ("zb",) + ANGLE, 0, 0, tiled=True)
    own, other = project(yh.reshape(1), co.reshape(1), both, k2, d)
    parts = own + lax.ppermute(other, "co", [(0, 1), (1, 0)])
    parts = lax.all_to_all(parts, ("yl", "x"), 0, 0, tiled=True)
    out = lax.all_to_all(fold(parts), Z, 0, 0, tiled=True)
    out = out.reshape(NZ, -1)[:, : VIEWS * NB].reshape(NZ, VIEWS, NB)
    return out.transpose(1, 0, 2).reshape(1, VIEWS, NZ * NB)


def solution(mesh):
    own = Mesh(mesh.devices.reshape(8, 2, 2, 2, 4, 2), CUTS + ANGLE)
    return jax.shard_map(
        local,
        mesh=own,
        in_specs=(P(CUTS, ANGLE, None), P(CUTS, None, None)),
        out_specs=P(CUTS, ANGLE, None),
        check_vma=False,
    )
```

```python
import jax
import jax.numpy as jnp
from jax import lax
from jax.experimental import pallas as pl
from jax.experimental.pallas import tpu as pltpu
from jax.sharding import Mesh, PartitionSpec as P

Z = ("zp", "zb")
CUTS = Z + ("yh",)
ANGLE = ("yl", "x", "co")
NZ, NA, NR, NB = 16, 16, 16, 24
OFFSETS, VIEWS = 18, 36
ROWS, LANES = 16, 128
TAIL = OFFSETS * NB % LANES
PART = VIEWS // 2
F32, BF16 = jnp.float32, jnp.bfloat16
VMEM_BYTES = 40 << 20


def rotate(tile, shift):
    shift %= LANES
    return tile if shift == 0 else pltpu.roll(tile, shift, 1)


def assemble(count, pieces, rows=ROWS):
    lane = lax.broadcasted_iota(jnp.int32, (rows, LANES), 1)
    tiles, cache = [None] * count, {}
    for n, (get, src, dst, width) in enumerate(pieces):
        while width > 0:
            step = min(width, LANES - src % LANES, LANES - dst % LANES)
            key = (id(get), src // LANES, (dst - src) % LANES)
            if key not in cache:
                cache[key] = rotate(get(src // LANES), dst - src)
            t, at = dst // LANES, dst % LANES
            if tiles[t] is None or step == LANES:
                tiles[t] = cache[key]
            else:
                tiles[t] = jnp.where((lane >= at) & (lane < at + step), cache[key], tiles[t])
            src, dst, width = src + step, dst + step, width - step
    return tiles


def cached(load):
    seen = {}

    def get(t):
        if t not in seen:
            seen[t] = load(t)
        return seen[t]

    return get


def pack_kernel(mine_ref, yh_ref, k_hbm, d_hbm, o_ref, k_ref, d_ref, sems):
    radii = pl.ds(pl.multiple_of(mine_ref[0] * NR, NR), NR)
    copies = [
        pltpu.make_async_copy(k_hbm.at[:, radii, :], k_ref, sems.at[0]),
        pltpu.make_async_copy(d_hbm.at[0], d_ref, sems.at[1]),
    ]
    for copy in copies:
        copy.start()
    swap = yh_ref[0] == 1
    copies[1].wait()
    low, high = d_ref[:, :LANES].astype(F32), d_ref[:, LANES:].astype(F32)
    halves = jnp.where(swap, high, low), jnp.where(swap, low, high)
    rest = []
    for b in range(2):
        rows = [half[b * PART : (b + 1) * PART] for half in halves]
        for h in range(2):
            tile = rows[h][:ROWS].astype(BF16)
            for z in range(b, NZ, 2):
                o_ref[z, 4 + h] = tile
        parts = [rotate(rows[q // 2][ROWS:], (1 - q % 2) * LANES // 2) for q in range(4)]
        rest.append(jnp.concatenate(parts + [jnp.zeros((ROWS - 4 * (PART - ROWS), LANES), F32)], axis=0))
    copies[0].wait()
    readers = [
        cached(lambda t, l=l: k_ref[l, :, t * LANES : (t + 1) * LANES].astype(F32)) for l in range(OFFSETS)
    ]
    lane = lax.broadcasted_iota(jnp.int32, (ROWS, LANES), 1)
    for z in range(NZ):
        tiles = assemble(4, [(readers[l], z * NB, l * NB, NB) for l in range(OFFSETS)])
        for t in range(3):
            o_ref[z, t] = tiles[t].astype(BF16)
        o_ref[z, 3] = jnp.where(lane < TAIL, tiles[3], rest[z % 2]).astype(BF16)


def regroup_kernel(k_ref, d_ref, o_ref, swap_ref):
    per = LANES // NR
    lane = lax.broadcasted_iota(jnp.int32, (NZ, LANES), 1)
    masks = [(lane >= p * NR) & (lane < (p + 1) * NR) for p in range(per)]
    out = {}
    for angle in range(PART):
        t, p = divmod(angle, per)
        for a in range(NA):
            if angle < ROWS:
                tile, at = d_ref[1 + a // per, angle], a % per
            else:
                tile, at = d_ref[0, a // 4 * (PART - ROWS) + angle - ROWS], per // 2 + a % 4
            turned = rotate(tile, (p - at) * NR)
            out[a, t] = turned if (a, t) not in out else jnp.where(masks[p], turned, out[a, t])
    for (a, t), tile in out.items():
        for b in range(2):
            o_ref[b * NA + a, t] = tile
    for z in range(NZ):
        for t in range(3):
            swap_ref[z * 3 + t] = k_ref[z, t]
    for z in range(0, NZ, 2):
        swap_ref[NZ * 3 + z // 2] = jnp.where(lane < TAIL, k_ref[z, 3], rotate(k_ref[z + 1, 3], TAIL))


def main_kernel(yh_ref, co_ref, k1_ref, k2_ref, d_ref, own_ref, other_ref, flat, weights, paired, left):
    half = OFFSETS * NB
    group = NR * NB // LANES
    tiles_all = 2 * NZ * half // LANES
    blocks = tiles_all // group
    width = own_ref.shape[2]
    lane = lax.broadcasted_iota(jnp.int32, (ROWS, LANES), 1)
    first = yh_ref[0] == 0

    def reader(z, h):
        def load(t):
            a = k1_ref[z, t].astype(F32)
            b = k2_ref[z * 3 + t if t < 3 else NZ * 3 + z // 2].astype(F32)
            if t == 3 and z % 2:
                b = rotate(b, -TAIL)
            return jnp.where(first, a, b) if h == 0 else jnp.where(first, b, a)

        return cached(load)

    tiles = assemble(
        tiles_all, [(reader(z, h), 0, (2 * z + h) * half, half) for z in range(NZ) for h in range(2)]
    )
    for t in range(tiles_all):
        flat[t + group] = tiles[t]
    for t in range(group):
        flat[t] = tiles[tiles_all - group + t]

    span = PART * NR
    tiles = assemble(
        blocks * 2,
        [
            (cached(lambda t, n=b * NA + a: d_ref[n, t].astype(F32)), 0, (2 * a + b) * span, span)
            for a in range(NA)
            for b in range(2)
        ],
    )
    for w in range(blocks):
        for t in range(2):
            tile = tiles[2 * w + t].astype(BF16)
            for rep in range(2):
                row = (rep * blocks + w) * NZ
                left[row : row + NZ, t * LANES : (t + 1) * LANES] = tile

    for block in range(blocks):
        for j in range(NR):
            q, rem = divmod(NB * j, LANES)
            base = block * group + group - q
            if rem:
                turned = [rotate(flat[base + t - 1], rem) for t in range(group + 1)]
                outs = [jnp.where(lane >= rem, turned[t + 1], turned[t]) for t in range(group)]
            else:
                outs = [flat[base + t] for t in range(group)]
            rows = slice(block * NR * NR + j * NR, block * NR * NR + (j + 1) * NR)
            for t in range(group - 1):
                weights[rows, t * LANES : (t + 1) * LANES] = outs[t].astype(BF16)
            pair, side = divmod(block, 2)
            rows = slice(pair * NR * NR + j * NR, pair * NR * NR + (j + 1) * NR)
            paired[rows, side * LANES : (side + 1) * LANES] = outs[group - 1].astype(BF16)
    lhs = [left[(blocks - c) * NZ : (2 * blocks - c) * NZ, :] for c in range(blocks)]
    acc = jnp.dot(jnp.concatenate(lhs, axis=1), weights[...], preferred_element_type=F32)
    last = jnp.dot(jnp.concatenate(lhs[::2], axis=1), paired[...], preferred_element_type=F32)

    def tile_of(t):
        u, t = divmod(t, group)
        if t < group - 1:
            return acc[u * NZ : (u + 1) * NZ, t * LANES : (t + 1) * LANES]
        before = (u - 1) % blocks
        return last[u * NZ : (u + 1) * NZ, :LANES] + last[before * NZ : (before + 1) * NZ, LANES:]

    out_tile = cached(tile_of)
    one = co_ref[0] == 1
    count = -(-width // LANES)
    for n in range(NA // 2):
        pair = [assemble(count, [(out_tile, a * width, 0, width)]) for a in (2 * n, 2 * n + 1)]
        for t in range(count):
            w = min(LANES, width - t * LANES)
            even, odd = (p[t][:, :w] for p in pair)
            own_ref[n, :, t * LANES : t * LANES + w] = jnp.where(one, odd, even)
            other_ref[n, :, t * LANES : t * LANES + w] = jnp.where(one, even, odd)


def fold_kernel(p_ref, o_ref, rows):
    def load(t):
        w = min(LANES, p_ref.shape[2] - t * LANES)
        tile = p_ref[0, :, t * LANES : t * LANES + w]
        for n in range(1, p_ref.shape[0]):
            tile = tile + p_ref[n, :, t * LANES : t * LANES + w]
        return tile if w == LANES else jnp.concatenate([tile, jnp.zeros((NZ, LANES - w), F32)], axis=1)

    get = cached(load)
    for i in range(8):
        pieces = [(get, v * NB, v // 8 * NB, NB) for v in range(i, VIEWS, 8)]
        rows[:, i, :] = assemble(1, pieces)[0]
    o_ref[...] = rows[...].astype(BF16)


def place_kernel(t_ref, o_ref):
    readers = [cached(lambda t, z=z: t_ref[z].astype(F32)) for z in range(NZ)]
    for first in range(0, VIEWS, 8):
        count = min(8, VIEWS - first)
        tiles = assemble(NZ * NB // LANES, [(readers[z], first // 8 * NB, z * NB, NB) for z in range(NZ)], 8)
        for t, tile in enumerate(tiles):
            o_ref[0, first : first + count, t * LANES : (t + 1) * LANES] = tile[:count].astype(BF16)


def pack(mine, yh, kernel_blocks, density):
    hbm, smem = pl.BlockSpec(memory_space=pltpu.HBM), pl.BlockSpec(memory_space=pltpu.SMEM)
    return pl.pallas_call(
        pack_kernel,
        in_specs=[smem, smem, hbm, hbm],
        out_specs=pl.BlockSpec(memory_space=pltpu.VMEM),
        out_shape=jax.ShapeDtypeStruct((NZ, 6, ROWS, LANES), BF16),
        scratch_shapes=[
            pltpu.VMEM((OFFSETS, NR, NZ * NB), BF16),
            pltpu.VMEM((VIEWS, NA * NR), BF16),
            pltpu.SemaphoreType.DMA((2,)),
        ],
        compiler_params=pltpu.CompilerParams(vmem_limit_bytes=VMEM_BYTES),
        name="pack",
    )(mine, yh, *(pltpu.with_memory_space_constraint(v, pltpu.HBM) for v in (kernel_blocks, density)))


def regroup(both):
    vmem = pl.BlockSpec(memory_space=pltpu.VMEM)
    d = both[:, 3:].transpose(1, 2, 0, 3)
    return pl.pallas_call(
        regroup_kernel,
        in_specs=[vmem, vmem],
        out_specs=[vmem, vmem],
        out_shape=[
            jax.ShapeDtypeStruct((2 * NA, d.shape[0], NZ, LANES), BF16),
            jax.ShapeDtypeStruct((NZ * 3 + NZ // 2, ROWS, LANES), BF16),
        ],
        compiler_params=pltpu.CompilerParams(vmem_limit_bytes=VMEM_BYTES),
        name="regroup",
    )(both, d)


def project(yh, co, k1, k2, d):
    half = OFFSETS * NB
    blocks = 2 * NZ * half // (NR * NB)
    width = 2 * NZ * half // NA
    smem, vmem = pl.BlockSpec(memory_space=pltpu.SMEM), pl.BlockSpec(memory_space=pltpu.VMEM)
    return pl.pallas_call(
        main_kernel,
        in_specs=[smem, smem, vmem, vmem, vmem],
        out_specs=[vmem, vmem],
        out_shape=[jax.ShapeDtypeStruct((NA // 2, NZ, width), F32)] * 2,
        scratch_shapes=[
            pltpu.VMEM((2 * NZ * half // LANES + NR * NB // LANES, ROWS, LANES), F32),
            pltpu.VMEM((blocks * NR * NR, 2 * LANES), BF16),
            pltpu.VMEM((blocks // 2 * NR * NR, 2 * LANES), BF16),
            pltpu.VMEM((2 * blocks * NZ, NR * NR), BF16),
        ],
        compiler_params=pltpu.CompilerParams(vmem_limit_bytes=VMEM_BYTES),
        name="project",
    )(yh, co, k1, k2, d)


def fold(parts):
    vmem = pl.BlockSpec(memory_space=pltpu.VMEM)
    return pl.pallas_call(
        fold_kernel,
        in_specs=[vmem],
        out_specs=vmem,
        out_shape=jax.ShapeDtypeStruct((NZ, 8, LANES), BF16),
        scratch_shapes=[pltpu.VMEM((NZ, 8, LANES), F32)],
        compiler_params=pltpu.CompilerParams(vmem_limit_bytes=VMEM_BYTES),
        name="fold",
    )(parts)


def place(tiles):
    vmem = pl.BlockSpec(memory_space=pltpu.VMEM)
    return pl.pallas_call(
        place_kernel,
        in_specs=[vmem],
        out_specs=vmem,
        out_shape=jax.ShapeDtypeStruct((1, VIEWS, NZ * NB), BF16),
        compiler_params=pltpu.CompilerParams(vmem_limit_bytes=VMEM_BYTES),
        name="place",
    )(tiles)


def local(density, kernel_blocks):
    yh, yl, x, co = (lax.axis_index(name).astype(jnp.int32) for name in ("yh",) + ANGLE)
    mine = ((yl ^ yh) * 4 + x) * 2 + co
    both = lax.all_to_all(pack(mine.reshape(1), yh.reshape(1), kernel_blocks, density), Z, 0, 0, tiled=True)
    d, k2 = regroup(both)
    k2 = lax.ppermute(k2, ("yh", "yl"), [(0, 3), (1, 2), (2, 1), (3, 0)])
    d = lax.all_to_all(d, ("zb",) + ANGLE, 0, 0, tiled=True)
    own, other = project(yh.reshape(1), co.reshape(1), both, k2, d)
    parts = own + lax.ppermute(other, "co", [(0, 1), (1, 0)])
    parts = lax.all_to_all(parts, ("yl", "x"), 0, 0, tiled=True)
    return place(lax.all_to_all(fold(parts), Z, 0, 0, tiled=True))


def solution(mesh):
    own = Mesh(mesh.devices.reshape(8, 2, 2, 2, 4, 2), CUTS + ANGLE)
    return jax.shard_map(
        local,
        mesh=own,
        in_specs=(P(CUTS, ANGLE, None), P(CUTS, None, None)),
        out_specs=P(CUTS, ANGLE, None),
        check_vma=False,
    )
```

```python
import jax
import jax.numpy as jnp
from jax import lax
from jax.experimental import pallas as pl
from jax.experimental.pallas import tpu as pltpu
from jax.sharding import Mesh, PartitionSpec as P

Z = ("zp", "zb")
CUTS = Z + ("yh",)
ANGLE = ("yl", "x", "co")
NZ, NA, NR, NB = 16, 16, 16, 24
OFFSETS, VIEWS = 18, 36
ROWS, LANES = 16, 128
TAIL = OFFSETS * NB % LANES
PART = VIEWS // 2
F32, BF16 = jnp.float32, jnp.bfloat16
VMEM_BYTES = 40 << 20


def rotate(tile, shift):
    shift %= LANES
    return tile if shift == 0 else pltpu.roll(tile, shift, 1)


def assemble(count, pieces, rows=ROWS):
    lane = lax.broadcasted_iota(jnp.int32, (rows, LANES), 1)
    tiles, cache = [None] * count, {}
    for n, (get, src, dst, width) in enumerate(pieces):
        while width > 0:
            step = min(width, LANES - src % LANES, LANES - dst % LANES)
            key = (id(get), src // LANES, (dst - src) % LANES)
            if key not in cache:
                cache[key] = rotate(get(src // LANES), dst - src)
            t, at = dst // LANES, dst % LANES
            if tiles[t] is None or step == LANES:
                tiles[t] = cache[key]
            else:
                tiles[t] = jnp.where((lane >= at) & (lane < at + step), cache[key], tiles[t])
            src, dst, width = src + step, dst + step, width - step
    return tiles


def cached(load):
    seen = {}

    def get(t):
        if t not in seen:
            seen[t] = load(t)
        return seen[t]

    return get


def pack_kernel(mine_ref, yh_ref, k_hbm, d_hbm, o_ref, k_ref, d_ref, sems):
    radii = pl.ds(pl.multiple_of(mine_ref[0] * NR, NR), NR)
    copies = [
        pltpu.make_async_copy(k_hbm.at[:, radii, :], k_ref, sems.at[0]),
        pltpu.make_async_copy(d_hbm.at[0], d_ref, sems.at[1]),
    ]
    for copy in copies:
        copy.start()
    swap = yh_ref[0] == 1
    copies[1].wait()
    low, high = d_ref[:, :LANES].astype(F32), d_ref[:, LANES:].astype(F32)
    halves = jnp.where(swap, high, low), jnp.where(swap, low, high)
    rest = []
    for b in range(2):
        rows = [half[b * PART : (b + 1) * PART] for half in halves]
        for h in range(2):
            tile = rows[h][:ROWS].astype(BF16)
            for z in range(b, NZ, 2):
                o_ref[z, 4 + h] = tile
        parts = [rotate(rows[q // 2][ROWS:], (1 - q % 2) * LANES // 2) for q in range(4)]
        rest.append(jnp.concatenate(parts + [jnp.zeros((ROWS - 4 * (PART - ROWS), LANES), F32)], axis=0))
    copies[0].wait()
    readers = [
        cached(lambda t, l=l: k_ref[l, :, t * LANES : (t + 1) * LANES].astype(F32)) for l in range(OFFSETS)
    ]
    lane = lax.broadcasted_iota(jnp.int32, (ROWS, LANES), 1)
    for z in range(NZ):
        tiles = assemble(4, [(readers[l], z * NB, l * NB, NB) for l in range(OFFSETS)])
        for t in range(3):
            o_ref[z, t] = tiles[t].astype(BF16)
        o_ref[z, 3] = jnp.where(lane < TAIL, tiles[3], rest[z % 2]).astype(BF16)


def regroup_kernel(k_ref, d_ref, o_ref, swap_ref):
    per = LANES // NR
    lane = lax.broadcasted_iota(jnp.int32, (NZ, LANES), 1)
    masks = [(lane >= p * NR) & (lane < (p + 1) * NR) for p in range(per)]
    out = {}
    for angle in range(PART):
        t, p = divmod(angle, per)
        for a in range(NA):
            if angle < ROWS:
                tile, at = d_ref[1 + a // per, angle], a % per
            else:
                tile, at = d_ref[0, a // 4 * (PART - ROWS) + angle - ROWS], per // 2 + a % 4
            turned = rotate(tile, (p - at) * NR)
            out[a, t] = turned if (a, t) not in out else jnp.where(masks[p], turned, out[a, t])
    for (a, t), tile in out.items():
        for b in range(2):
            o_ref[b * NA + a, t] = tile
    for z in range(NZ):
        for t in range(3):
            swap_ref[z * 3 + t] = k_ref[z, t]
    for z in range(0, NZ, 2):
        swap_ref[NZ * 3 + z // 2] = jnp.where(lane < TAIL, k_ref[z, 3], rotate(k_ref[z + 1, 3], TAIL))


def rows_kernel(d_ref, left):
    blocks = left.shape[0] // (2 * NZ)
    span = PART * NR
    tiles = assemble(
        blocks * 2,
        [
            (cached(lambda t, n=b * NA + a: d_ref[n, t].astype(F32)), 0, (2 * a + b) * span, span)
            for a in range(NA)
            for b in range(2)
        ],
    )
    for w in range(blocks):
        for t in range(2):
            tile = tiles[2 * w + t].astype(BF16)
            for rep in range(2):
                row = (rep * blocks + w) * NZ
                left[row : row + NZ, t * LANES : (t + 1) * LANES] = tile


def main_kernel(yh_ref, co_ref, k1_ref, k2_ref, left, own_ref, other_ref, flat, weights, paired):
    half = OFFSETS * NB
    group = NR * NB // LANES
    tiles_all = 2 * NZ * half // LANES
    blocks = tiles_all // group
    width = own_ref.shape[2]
    lane = lax.broadcasted_iota(jnp.int32, (ROWS, LANES), 1)
    first = yh_ref[0] == 0

    def reader(z, h):
        def load(t):
            a = k1_ref[z, t].astype(F32)
            b = k2_ref[z * 3 + t if t < 3 else NZ * 3 + z // 2].astype(F32)
            if t == 3 and z % 2:
                b = rotate(b, -TAIL)
            return jnp.where(first, a, b) if h == 0 else jnp.where(first, b, a)

        return cached(load)

    tiles = assemble(
        tiles_all, [(reader(z, h), 0, (2 * z + h) * half, half) for z in range(NZ) for h in range(2)]
    )
    for t in range(tiles_all):
        flat[t + group] = tiles[t]
    for t in range(group):
        flat[t] = tiles[tiles_all - group + t]

    for block in range(blocks):
        for j in range(NR):
            q, rem = divmod(NB * j, LANES)
            base = block * group + group - q
            if rem:
                turned = [rotate(flat[base + t - 1], rem) for t in range(group + 1)]
                outs = [jnp.where(lane >= rem, turned[t + 1], turned[t]) for t in range(group)]
            else:
                outs = [flat[base + t] for t in range(group)]
            rows = slice(block * NR * NR + j * NR, block * NR * NR + (j + 1) * NR)
            for t in range(group - 1):
                weights[rows, t * LANES : (t + 1) * LANES] = outs[t].astype(BF16)
            pair, side = divmod(block, 2)
            rows = slice(pair * NR * NR + j * NR, pair * NR * NR + (j + 1) * NR)
            paired[rows, side * LANES : (side + 1) * LANES] = outs[group - 1].astype(BF16)
    lhs = [left[(blocks - c) * NZ : (2 * blocks - c) * NZ, :] for c in range(blocks)]
    acc = jnp.dot(jnp.concatenate(lhs, axis=1), weights[...], preferred_element_type=F32)
    last = jnp.dot(jnp.concatenate(lhs[::2], axis=1), paired[...], preferred_element_type=F32)

    def tile_of(t):
        u, t = divmod(t, group)
        if t < group - 1:
            return acc[u * NZ : (u + 1) * NZ, t * LANES : (t + 1) * LANES]
        before = (u - 1) % blocks
        return last[u * NZ : (u + 1) * NZ, :LANES] + last[before * NZ : (before + 1) * NZ, LANES:]

    out_tile = cached(tile_of)
    one = co_ref[0] == 1
    count = -(-width // LANES)
    for n in range(NA // 2):
        pair = [assemble(count, [(out_tile, a * width, 0, width)]) for a in (2 * n, 2 * n + 1)]
        for t in range(count):
            w = min(LANES, width - t * LANES)
            even, odd = (p[t][:, :w] for p in pair)
            own_ref[n, :, t * LANES : t * LANES + w] = jnp.where(one, odd, even)
            other_ref[n, :, t * LANES : t * LANES + w] = jnp.where(one, even, odd)


def fold_kernel(p_ref, o_ref, rows):
    def load(t):
        w = min(LANES, p_ref.shape[2] - t * LANES)
        tile = p_ref[0, :, t * LANES : t * LANES + w]
        for n in range(1, p_ref.shape[0]):
            tile = tile + p_ref[n, :, t * LANES : t * LANES + w]
        return tile if w == LANES else jnp.concatenate([tile, jnp.zeros((NZ, LANES - w), F32)], axis=1)

    get = cached(load)
    for i in range(8):
        pieces = [(get, v * NB, v // 8 * NB, NB) for v in range(i, VIEWS, 8)]
        rows[:, i, :] = assemble(1, pieces)[0]
    o_ref[...] = rows[...].astype(BF16)


def place_kernel(t_ref, o_ref):
    readers = [cached(lambda t, z=z: t_ref[z].astype(F32)) for z in range(NZ)]
    for first in range(0, VIEWS, 8):
        count = min(8, VIEWS - first)
        tiles = assemble(NZ * NB // LANES, [(readers[z], first // 8 * NB, z * NB, NB) for z in range(NZ)], 8)
        for t, tile in enumerate(tiles):
            o_ref[0, first : first + count, t * LANES : (t + 1) * LANES] = tile[:count].astype(BF16)


def pack(mine, yh, kernel_blocks, density):
    hbm, smem = pl.BlockSpec(memory_space=pltpu.HBM), pl.BlockSpec(memory_space=pltpu.SMEM)
    return pl.pallas_call(
        pack_kernel,
        in_specs=[smem, smem, hbm, hbm],
        out_specs=pl.BlockSpec(memory_space=pltpu.VMEM),
        out_shape=jax.ShapeDtypeStruct((NZ, 6, ROWS, LANES), BF16),
        scratch_shapes=[
            pltpu.VMEM((OFFSETS, NR, NZ * NB), BF16),
            pltpu.VMEM((VIEWS, NA * NR), BF16),
            pltpu.SemaphoreType.DMA((2,)),
        ],
        compiler_params=pltpu.CompilerParams(vmem_limit_bytes=VMEM_BYTES),
        name="pack",
    )(mine, yh, *(pltpu.with_memory_space_constraint(v, pltpu.HBM) for v in (kernel_blocks, density)))


def regroup(both):
    vmem = pl.BlockSpec(memory_space=pltpu.VMEM)
    d = both[:, 3:].transpose(1, 2, 0, 3)
    return pl.pallas_call(
        regroup_kernel,
        in_specs=[vmem, vmem],
        out_specs=[vmem, vmem],
        out_shape=[
            jax.ShapeDtypeStruct((2 * NA, d.shape[0], NZ, LANES), BF16),
            jax.ShapeDtypeStruct((NZ * 3 + NZ // 2, ROWS, LANES), BF16),
        ],
        compiler_params=pltpu.CompilerParams(vmem_limit_bytes=VMEM_BYTES),
        name="regroup",
    )(both, d)


def density_rows(d):
    vmem = pl.BlockSpec(memory_space=pltpu.VMEM)
    return pl.pallas_call(
        rows_kernel,
        in_specs=[vmem],
        out_specs=vmem,
        out_shape=jax.ShapeDtypeStruct((2 * NA * VIEWS * NZ // NR, NR * NR), BF16),
        compiler_params=pltpu.CompilerParams(vmem_limit_bytes=VMEM_BYTES),
        name="density_rows",
    )(d)


def project(yh, co, k1, k2, d):
    half = OFFSETS * NB
    blocks = 2 * NZ * half // (NR * NB)
    width = 2 * NZ * half // NA
    smem, vmem = pl.BlockSpec(memory_space=pltpu.SMEM), pl.BlockSpec(memory_space=pltpu.VMEM)
    return pl.pallas_call(
        main_kernel,
        in_specs=[smem, smem, vmem, vmem, vmem],
        out_specs=[vmem, vmem],
        out_shape=[jax.ShapeDtypeStruct((NA // 2, NZ, width), F32)] * 2,
        scratch_shapes=[
            pltpu.VMEM((2 * NZ * half // LANES + NR * NB // LANES, ROWS, LANES), F32),
            pltpu.VMEM((blocks * NR * NR, 2 * LANES), BF16),
            pltpu.VMEM((blocks // 2 * NR * NR, 2 * LANES), BF16),
        ],
        compiler_params=pltpu.CompilerParams(vmem_limit_bytes=VMEM_BYTES),
        name="project",
    )(yh, co, k1, k2, d)


def fold(parts):
    vmem = pl.BlockSpec(memory_space=pltpu.VMEM)
    return pl.pallas_call(
        fold_kernel,
        in_specs=[vmem],
        out_specs=vmem,
        out_shape=jax.ShapeDtypeStruct((NZ, 8, LANES), BF16),
        scratch_shapes=[pltpu.VMEM((NZ, 8, LANES), F32)],
        compiler_params=pltpu.CompilerParams(vmem_limit_bytes=VMEM_BYTES),
        name="fold",
    )(parts)


def place(tiles):
    vmem = pl.BlockSpec(memory_space=pltpu.VMEM)
    return pl.pallas_call(
        place_kernel,
        in_specs=[vmem],
        out_specs=vmem,
        out_shape=jax.ShapeDtypeStruct((1, VIEWS, NZ * NB), BF16),
        compiler_params=pltpu.CompilerParams(vmem_limit_bytes=VMEM_BYTES),
        name="place",
    )(tiles)


def local(density, kernel_blocks):
    yh, yl, x, co = (lax.axis_index(name).astype(jnp.int32) for name in ("yh",) + ANGLE)
    mine = ((yl ^ yh) * 4 + x) * 2 + co
    both = lax.all_to_all(pack(mine.reshape(1), yh.reshape(1), kernel_blocks, density), Z, 0, 0, tiled=True)
    d, k2 = regroup(both)
    k2 = lax.ppermute(k2, ("yh", "yl"), [(0, 3), (1, 2), (2, 1), (3, 0)])
    d = lax.all_to_all(d, ("zb",) + ANGLE, 0, 0, tiled=True)
    own, other = project(yh.reshape(1), co.reshape(1), both, k2, density_rows(d))
    parts = own + lax.ppermute(other, "co", [(0, 1), (1, 0)])
    parts = lax.all_to_all(parts, ("yl", "x"), 0, 0, tiled=True)
    return place(lax.all_to_all(fold(parts), Z, 0, 0, tiled=True))


def solution(mesh):
    own = Mesh(mesh.devices.reshape(8, 2, 2, 2, 4, 2), CUTS + ANGLE)
    return jax.shard_map(
        local,
        mesh=own,
        in_specs=(P(CUTS, ANGLE, None), P(CUTS, None, None)),
        out_specs=P(CUTS, ANGLE, None),
        check_vma=False,
    )
```

```python
import jax
import jax.numpy as jnp
from jax import lax
from jax.experimental import pallas as pl
from jax.experimental.pallas import tpu as pltpu
from jax.sharding import Mesh, PartitionSpec as P

Z = ("zp", "zb")
CUTS = Z + ("yh",)
ANGLE = ("yl", "x", "co")
NZ, NA, NR, NB = 16, 16, 16, 24
OFFSETS, VIEWS = 18, 36
ROWS, LANES = 16, 128
TAIL = OFFSETS * NB % LANES
PART = VIEWS // 2
F32, BF16 = jnp.float32, jnp.bfloat16
VMEM_BYTES = 40 << 20


def rotate(tile, shift):
    shift %= LANES
    return tile if shift == 0 else pltpu.roll(tile, shift, 1)


def assemble(count, pieces, rows=ROWS):
    lane = lax.broadcasted_iota(jnp.int32, (rows, LANES), 1)
    tiles, cache = [None] * count, {}
    for n, (get, src, dst, width) in enumerate(pieces):
        while width > 0:
            step = min(width, LANES - src % LANES, LANES - dst % LANES)
            key = (id(get), src // LANES, (dst - src) % LANES)
            if key not in cache:
                cache[key] = rotate(get(src // LANES), dst - src)
            t, at = dst // LANES, dst % LANES
            if tiles[t] is None or step == LANES:
                tiles[t] = cache[key]
            else:
                tiles[t] = jnp.where((lane >= at) & (lane < at + step), cache[key], tiles[t])
            src, dst, width = src + step, dst + step, width - step
    return tiles


def cached(load):
    seen = {}

    def get(t):
        if t not in seen:
            seen[t] = load(t)
        return seen[t]

    return get


def pack_kernel(mine_ref, yh_ref, k_hbm, d_hbm, o_ref, k_ref, d_ref, sems):
    radii = pl.ds(pl.multiple_of(mine_ref[0] * NR, NR), NR)
    copies = [
        pltpu.make_async_copy(k_hbm.at[:, radii, :], k_ref, sems.at[0]),
        pltpu.make_async_copy(d_hbm.at[0], d_ref, sems.at[1]),
    ]
    for copy in copies:
        copy.start()
    swap = yh_ref[0] == 1
    copies[1].wait()
    low, high = d_ref[:, :LANES].astype(F32), d_ref[:, LANES:].astype(F32)
    halves = jnp.where(swap, high, low), jnp.where(swap, low, high)
    rest = []
    for b in range(2):
        rows = [half[b * PART : (b + 1) * PART] for half in halves]
        for h in range(2):
            tile = rows[h][:ROWS].astype(BF16)
            for z in range(b, NZ, 2):
                o_ref[z, 4 + h] = tile
        parts = [rotate(rows[q // 2][ROWS:], (1 - q % 2) * LANES // 2) for q in range(4)]
        rest.append(jnp.concatenate(parts + [jnp.zeros((ROWS - 4 * (PART - ROWS), LANES), F32)], axis=0))
    copies[0].wait()
    readers = [
        cached(lambda t, l=l: k_ref[l, :, t * LANES : (t + 1) * LANES].astype(F32)) for l in range(OFFSETS)
    ]
    lane = lax.broadcasted_iota(jnp.int32, (ROWS, LANES), 1)
    for z in range(NZ):
        tiles = assemble(4, [(readers[l], z * NB, l * NB, NB) for l in range(OFFSETS)])
        for t in range(3):
            o_ref[z, t] = tiles[t].astype(BF16)
        o_ref[z, 3] = jnp.where(lane < TAIL, tiles[3], rest[z % 2]).astype(BF16)


def regroup_kernel(k_ref, d_ref, o_ref, swap_ref):
    per = LANES // NR
    lane = lax.broadcasted_iota(jnp.int32, (NZ, LANES), 1)
    masks = [(lane >= p * NR) & (lane < (p + 1) * NR) for p in range(per)]
    out = {}
    for angle in range(PART):
        t, p = divmod(angle, per)
        for a in range(NA):
            if angle < ROWS:
                tile, at = d_ref[1 + a // per, angle], a % per
            else:
                tile, at = d_ref[0, a // 4 * (PART - ROWS) + angle - ROWS], per // 2 + a % 4
            turned = rotate(tile, (p - at) * NR)
            out[a, t] = turned if (a, t) not in out else jnp.where(masks[p], turned, out[a, t])
    for (a, t), tile in out.items():
        for b in range(2):
            o_ref[b * NA + a, t] = tile
    for z in range(NZ):
        for t in range(3):
            swap_ref[z * 3 + t] = k_ref[z, t]
    for z in range(0, NZ, 2):
        swap_ref[NZ * 3 + z // 2] = jnp.where(lane < TAIL, k_ref[z, 3], rotate(k_ref[z + 1, 3], TAIL))


def main_kernel(yh_ref, co_ref, k1_ref, k2_ref, d_ref, own_ref, other_ref, flat, weights, paired, left):
    half = OFFSETS * NB
    group = NR * NB // LANES
    tiles_all = 2 * NZ * half // LANES
    blocks = tiles_all // group
    width = own_ref.shape[2]
    lane = lax.broadcasted_iota(jnp.int32, (ROWS, LANES), 1)
    first = yh_ref[0] == 0

    def reader(z, h):
        def load(t):
            a = k1_ref[z, t].astype(F32)
            b = k2_ref[z * 3 + t if t < 3 else NZ * 3 + z // 2].astype(F32)
            if t == 3 and z % 2:
                b = rotate(b, -TAIL)
            return jnp.where(first, a, b) if h == 0 else jnp.where(first, b, a)

        return cached(load)

    tiles = assemble(
        tiles_all, [(reader(z, h), 0, (2 * z + h) * half, half) for z in range(NZ) for h in range(2)]
    )
    for t in range(tiles_all):
        flat[t + group] = tiles[t]
    for t in range(group):
        flat[t] = tiles[tiles_all - group + t]

    span = PART * NR
    tiles = assemble(
        blocks * 2,
        [
            (cached(lambda t, n=b * NA + a: d_ref[n, t].astype(F32)), 0, (2 * a + b) * span, span)
            for a in range(NA)
            for b in range(2)
        ],
    )
    for w in range(blocks):
        for t in range(2):
            tile = tiles[2 * w + t].astype(BF16)
            for rep in range(2):
                row = (rep * blocks + w) * NZ
                left[row : row + NZ, t * LANES : (t + 1) * LANES] = tile

    for block in range(blocks):
        for j in range(NR):
            q, rem = divmod(NB * j, LANES)
            base = block * group + group - q
            if rem:
                turned = [rotate(flat[base + t - 1], rem) for t in range(group + 1)]
                outs = [jnp.where(lane >= rem, turned[t + 1], turned[t]) for t in range(group)]
            else:
                outs = [flat[base + t] for t in range(group)]
            rows = slice(block * NR * NR + j * NR, block * NR * NR + (j + 1) * NR)
            for t in range(group - 1):
                weights[rows, t * LANES : (t + 1) * LANES] = outs[t].astype(BF16)
            pair, side = divmod(block, 2)
            rows = slice(pair * NR * NR + j * NR, pair * NR * NR + (j + 1) * NR)
            paired[rows, side * LANES : (side + 1) * LANES] = outs[group - 1].astype(BF16)
    lhs = [left[(blocks - c) * NZ : (2 * blocks - c) * NZ, :] for c in range(blocks)]
    acc = jnp.dot(jnp.concatenate(lhs, axis=1), weights[...], preferred_element_type=F32)
    last = jnp.dot(jnp.concatenate(lhs[::2], axis=1), paired[...], preferred_element_type=F32)

    def tile_of(t):
        u, t = divmod(t, group)
        if t < group - 1:
            return acc[u * NZ : (u + 1) * NZ, t * LANES : (t + 1) * LANES]
        before = (u - 1) % blocks
        return last[u * NZ : (u + 1) * NZ, :LANES] + last[before * NZ : (before + 1) * NZ, LANES:]

    out_tile = cached(tile_of)
    one = co_ref[0] == 1
    count = -(-width // LANES)
    for n in range(NA // 2):
        pair = [assemble(count, [(out_tile, a * width, 0, width)]) for a in (2 * n, 2 * n + 1)]
        for t in range(count):
            w = min(LANES, width - t * LANES)
            even, odd = (p[t][:, :w] for p in pair)
            own_ref[n % 4 * 2 + n // 4, :, t * LANES : t * LANES + w] = jnp.where(one, odd, even)
            other_ref[n % 4 * 2 + n // 4, :, t * LANES : t * LANES + w] = jnp.where(one, even, odd)


def fold_kernel(p_ref, o_ref, rows):
    def load(t):
        w = min(LANES, p_ref.shape[2] - t * LANES)
        tile = p_ref[0, :, t * LANES : t * LANES + w]
        for n in range(1, p_ref.shape[0]):
            tile = tile + p_ref[n, :, t * LANES : t * LANES + w]
        return tile if w == LANES else jnp.concatenate([tile, jnp.zeros((NZ, LANES - w), F32)], axis=1)

    get = cached(load)
    for i in range(8):
        pieces = [(get, v * NB, v // 8 * NB, NB) for v in range(i, VIEWS, 8)]
        rows[:, i, :] = assemble(1, pieces)[0]
    o_ref[...] = rows[...].astype(BF16)


def place_kernel(t_ref, o_ref):
    readers = [cached(lambda t, z=z: t_ref[z].astype(F32)) for z in range(NZ)]
    for first in range(0, VIEWS, 8):
        count = min(8, VIEWS - first)
        tiles = assemble(NZ * NB // LANES, [(readers[z], first // 8 * NB, z * NB, NB) for z in range(NZ)], 8)
        for t, tile in enumerate(tiles):
            o_ref[0, first : first + count, t * LANES : (t + 1) * LANES] = tile[:count].astype(BF16)


def pack(mine, yh, kernel_blocks, density):
    hbm, smem = pl.BlockSpec(memory_space=pltpu.HBM), pl.BlockSpec(memory_space=pltpu.SMEM)
    return pl.pallas_call(
        pack_kernel,
        in_specs=[smem, smem, hbm, hbm],
        out_specs=pl.BlockSpec(memory_space=pltpu.VMEM),
        out_shape=jax.ShapeDtypeStruct((NZ, 6, ROWS, LANES), BF16),
        scratch_shapes=[
            pltpu.VMEM((OFFSETS, NR, NZ * NB), BF16),
            pltpu.VMEM((VIEWS, NA * NR), BF16),
            pltpu.SemaphoreType.DMA((2,)),
        ],
        compiler_params=pltpu.CompilerParams(vmem_limit_bytes=VMEM_BYTES),
        name="pack",
    )(mine, yh, *(pltpu.with_memory_space_constraint(v, pltpu.HBM) for v in (kernel_blocks, density)))


def regroup(both):
    vmem = pl.BlockSpec(memory_space=pltpu.VMEM)
    d = both[:, 3:].transpose(1, 2, 0, 3)
    return pl.pallas_call(
        regroup_kernel,
        in_specs=[vmem, vmem],
        out_specs=[vmem, vmem],
        out_shape=[
            jax.ShapeDtypeStruct((2 * NA, d.shape[0], NZ, LANES), BF16),
            jax.ShapeDtypeStruct((NZ * 3 + NZ // 2, ROWS, LANES), BF16),
        ],
        compiler_params=pltpu.CompilerParams(vmem_limit_bytes=VMEM_BYTES),
        name="regroup",
    )(both, d)


def project(yh, co, k1, k2, d):
    half = OFFSETS * NB
    blocks = 2 * NZ * half // (NR * NB)
    width = 2 * NZ * half // NA
    smem, vmem = pl.BlockSpec(memory_space=pltpu.SMEM), pl.BlockSpec(memory_space=pltpu.VMEM)
    return pl.pallas_call(
        main_kernel,
        in_specs=[smem, smem, vmem, vmem, vmem],
        out_specs=[vmem, vmem],
        out_shape=[jax.ShapeDtypeStruct((NA // 2, NZ, width), F32)] * 2,
        scratch_shapes=[
            pltpu.VMEM((2 * NZ * half // LANES + NR * NB // LANES, ROWS, LANES), F32),
            pltpu.VMEM((blocks * NR * NR, 2 * LANES), BF16),
            pltpu.VMEM((blocks // 2 * NR * NR, 2 * LANES), BF16),
            pltpu.VMEM((2 * blocks * NZ, NR * NR), BF16),
        ],
        compiler_params=pltpu.CompilerParams(vmem_limit_bytes=VMEM_BYTES),
        name="project",
    )(yh, co, k1, k2, d)


def fold(parts):
    vmem = pl.BlockSpec(memory_space=pltpu.VMEM)
    return pl.pallas_call(
        fold_kernel,
        in_specs=[vmem],
        out_specs=vmem,
        out_shape=jax.ShapeDtypeStruct((NZ, 8, LANES), BF16),
        scratch_shapes=[pltpu.VMEM((NZ, 8, LANES), F32)],
        compiler_params=pltpu.CompilerParams(vmem_limit_bytes=VMEM_BYTES),
        name="fold",
    )(parts)


def place(tiles):
    vmem = pl.BlockSpec(memory_space=pltpu.VMEM)
    return pl.pallas_call(
        place_kernel,
        in_specs=[vmem],
        out_specs=vmem,
        out_shape=jax.ShapeDtypeStruct((1, VIEWS, NZ * NB), BF16),
        compiler_params=pltpu.CompilerParams(vmem_limit_bytes=VMEM_BYTES),
        name="place",
    )(tiles)


def local(density, kernel_blocks):
    yh, yl, x, co = (lax.axis_index(name).astype(jnp.int32) for name in ("yh",) + ANGLE)
    mine = ((yl ^ yh) * 4 + x) * 2 + co
    both = lax.all_to_all(pack(mine.reshape(1), yh.reshape(1), kernel_blocks, density), Z, 0, 0, tiled=True)
    d, k2 = regroup(both)
    k2 = lax.ppermute(k2, ("yh", "yl"), [(0, 3), (1, 2), (2, 1), (3, 0)])
    d = lax.all_to_all(d, ("zb",) + ANGLE, 0, 0, tiled=True)
    own, other = project(yh.reshape(1), co.reshape(1), both, k2, d)
    parts = own + lax.ppermute(other, "co", [(0, 1), (1, 0)])
    parts = lax.all_to_all(parts, ("x", "yl"), 0, 0, tiled=True)
    return place(lax.all_to_all(fold(parts), Z, 0, 0, tiled=True))


def solution(mesh):
    own = Mesh(mesh.devices.reshape(8, 2, 2, 2, 4, 2), CUTS + ANGLE)
    return jax.shard_map(
        local,
        mesh=own,
        in_specs=(P(CUTS, ANGLE, None), P(CUTS, None, None)),
        out_specs=P(CUTS, ANGLE, None),
        check_vma=False,
    )
```
